32 devices in a mesh: walk: 4 (over x, core), pb: 8 (over z, y).
Axes of the slice: x: 2, y: 2, z: 4, core: 2. Of those that a mesh axis runs over, the one named last changes fastest.
Arguments:
- greens: bfloat16 [64, 64, 3072], P('walk', 'pb'), may hold values from -6 to 6
- cholesky: bfloat16 [32, 300, 3072], P('pb'), may hold values from -0.011962891 to 0.011962891
- slot_source: int32 [32], replicated, may hold values from 0 to 63, as said below
- block_transfer_index: int32 [32], P('pb'), may hold values from 0 to 15
- slot_multiplicity: int32 [32], P('pb'), may hold values from 0 to 3, as said below
- fields: float32 [64, 16, 300], P('walk'), may hold values from -6 to 6
- weight: float32 [64], P('walk'), may hold values from 0.2 to 5
Outputs:
- force_bias: float32 [64, 2, 4800], P('walk', None, 'pb')
- local_energy: float32 [64], P('walk')
- new_weight: float32 [64], P('walk')
- mixed_energy: float32 [], replicated
The draws below stay inside these ranges and needn't reach their ends.
Inputs may be any that keep to these rules, and one draw needn't show every extreme that they name: `slot_source`: the Green's block of k-point k lies on index k // 8 of pb; with P = 8, slot j of pb index d (slot d * 4 + j) reads a block that lies on index (d + o_j) mod P of pb, where o_0 = 0, o_1 = P - 1, o_2 = 1, o_3 = P // 2. `slot_multiplicity`: 0 marks an empty slot; on each index of pb the live slots come first, and on some index all 4 slots are live.
All inputs are finite; a program needn't handle non-finite values.
Results may differ from the reference program's by a relative error of at most 0.0003.
Values may be sent and summed in bfloat16 or wider, within the bound.
A program may use at most 320 MiB of HBM per device.

```python
import math
import jax
import jax.numpy as jnp
from jax import lax

K = 64
ORBITAL_COUNT = 96
OCCUPIED_COUNT = 16
CHOLESKY_COUNT = 300
TRANSFER_COUNT = 16
PAIR_BLOCKS_HELD = 4
NW = 64
KPOINTS_PER_PART = 8
PAIR_BLOCK_TOTAL = 32


def draw_slot_source(key, part):
    group_list = PAIR_BLOCK_TOTAL // PAIR_BLOCKS_HELD
    offsets = jnp.array([0, group_list - 1, 1, group_list // 2], dtype=jnp.int32)
    owner_parts = (jnp.arange(group_list, dtype=jnp.int32)[:, None] + offsets[None, :]) % group_list
    within_group = jax.random.randint(jax.random.fold_in(key, 12), (group_list, PAIR_BLOCKS_HELD), 0, KPOINTS_PER_PART)
    return (owner_parts * KPOINTS_PER_PART + within_group).reshape(PAIR_BLOCK_TOTAL).astype(jnp.int32)


def draw_slot_multiplicity(key, part):
    group_list = PAIR_BLOCK_TOTAL // PAIR_BLOCKS_HELD
    first_draw = jax.random.randint(jax.random.fold_in(key, 21), (group_list,), 0, PAIR_BLOCKS_HELD)
    second_draw = jax.random.randint(jax.random.fold_in(key, 22), (group_list,), 0, PAIR_BLOCKS_HELD)
    live_count = 1 + first_draw * second_draw // max(PAIR_BLOCKS_HELD - 1, 1)
    full_index = jax.random.randint(jax.random.fold_in(key, 23), (), 0, group_list)
    live_count = jnp.where(jnp.arange(group_list) == full_index, PAIR_BLOCKS_HELD, live_count)
    levels = jax.random.randint(jax.random.fold_in(key, 24), (group_list, PAIR_BLOCKS_HELD), 1, 4)
    corner = (jnp.arange(group_list)[:, None] == full_index) & (jnp.arange(PAIR_BLOCKS_HELD)[None, :] == 0)
    levels = jnp.where(corner, 3, levels)
    multiple_count = jnp.where(jnp.arange(PAIR_BLOCKS_HELD)[None, :] < live_count[:, None], levels, 0)
    return multiple_count.reshape(PAIR_BLOCK_TOTAL).astype(jnp.int32)


def touch_ends(values, rng, least, largest):
    index_at = [jax.random.randint(jax.random.fold_in(rng, axis), (), 0, length) for axis, length in enumerate(values.shape)]
    longest = values.shape.index(max(values.shape))
    neighbour = index_at[:longest] + [(index_at[longest] + 1) % values.shape[longest]] + index_at[longest + 1:]
    return values.at[tuple(index_at)].set(least).at[tuple(neighbour)].set(largest)


def block_levels(stream_key, extent, split, low, high):
    def one(dim, shards_of):
        draws = jax.random.uniform(jax.random.fold_in(jax.random.fold_in(stream_key, 6), dim), (shards_of,), jnp.float32, low / len(split), high / len(split))
        return jnp.repeat(jnp.exp(draws), extent[dim] // shards_of).reshape((-1,) + (1,) * (len(extent) - dim - 1))

    gain = one(*split[0])
    for cut in split[1:]:
        gain = gain * one(*cut)
    return gain


def bell_draw(own_key, dims, spread, bound, cuts=(), held_as=jnp.bfloat16):
    level = block_levels(own_key, dims, cuts, -0.22, 0.18) if cuts else 1.0
    entries = jax.random.normal(own_key, dims, jnp.float32) * spread * level
    return jnp.minimum(jnp.maximum(entries, -bound), bound).astype(held_as)


def setup_inputs(seed: int = 0) -> dict:
    key_list = jax.random.split(jax.random.key(seed), 8)
    greens = bell_draw(key_list[0], (NW, K, OCCUPIED_COUNT * 2 * ORBITAL_COUNT), 1.0, 6.0, ((0, 4), (1, 8)))
    cholesky = bell_draw(key_list[1], (PAIR_BLOCK_TOTAL, CHOLESKY_COUNT, OCCUPIED_COUNT * 2 * ORBITAL_COUNT), 0.002, 0.011962891, ((0, 8),))
    slot_source = draw_slot_source(jax.random.fold_in(key_list[7], 71), 0)
    block_transfer_index = touch_ends(jax.random.randint(key_list[3], (PAIR_BLOCK_TOTAL,), 0, TRANSFER_COUNT), jax.random.fold_in(key_list[3], 1), 0, TRANSFER_COUNT - 1).astype(jnp.int32)
    slot_multiplicity = draw_slot_multiplicity(jax.random.fold_in(key_list[7], 71), 0)
    fields = bell_draw(key_list[5], (NW, TRANSFER_COUNT, CHOLESKY_COUNT), 1.0, 6.0, ((0, 4),), jnp.float32)
    weight = jnp.clip(jnp.exp(math.log(5.0) - 3.218876 * jax.random.uniform(key_list[6], (NW,), jnp.float32) ** block_levels(key_list[6], (NW,), ((0, 4),), -0.2, 0.2)), 0.2, 5.0)
    return dict(greens=greens, cholesky=cholesky, slot_source=slot_source, block_transfer_index=block_transfer_index, slot_multiplicity=slot_multiplicity, fields=fields, weight=weight)


sqrt_step = 0.05

def slot_terms(chol_flat, green_flat):
    vectors = chol_flat.shape[0]
    walkers = green_flat.shape[0]
    doubled = 2 * ORBITAL_COUNT
    chol_block = chol_flat.reshape(vectors, OCCUPIED_COUNT, doubled)
    green_rows = green_flat.reshape(walkers, OCCUPIED_COUNT, doubled)
    real_part = green_rows[..., :ORBITAL_COUNT]
    imag_part = green_rows[..., ORBITAL_COUNT:]
    stacked = jnp.stack([jnp.concatenate([real_part, -imag_part], -1), jnp.concatenate([imag_part, real_part], -1)], 0)
    left_matrix = chol_block.reshape(vectors * OCCUPIED_COUNT, doubled)
    right_matrix = stacked.reshape(2 * walkers * OCCUPIED_COUNT, doubled)
    product = jnp.dot(left_matrix, right_matrix.T, preferred_element_type=jnp.float32)
    product = product.reshape(vectors, OCCUPIED_COUNT, 2, walkers, OCCUPIED_COUNT)
    identity = jnp.eye(OCCUPIED_COUNT, dtype=jnp.float32)
    diagonal = jnp.einsum('nicwj,ij->wcn', product, identity)
    crossed = jnp.einsum('nicwj,njcwi->cw', product, product)
    return (diagonal, crossed[0] - crossed[1])

def reference(greens, cholesky, slot_source, block_transfer_index, slot_multiplicity, fields, weight):

    def advance(running, inputs):
        bias, exchange_sum = running
        chol_block, source, transfer, multiple_count = inputs
        green_rows = lax.dynamic_index_in_dim(greens, source.astype(jnp.int32), 1, keepdims=False)
        diagonal, crossed = slot_terms(chol_block, green_rows)
        scaled = multiple_count.astype(jnp.float32)
        factor = scaled * (jnp.arange(TRANSFER_COUNT) == transfer).astype(jnp.float32)
        bias = bias + factor[None, None, :, None] * diagonal[:, :, None, :]
        exchange_sum = exchange_sum + scaled * crossed
        return ((bias, exchange_sum), None)
    initial = (jnp.zeros((NW, 2, TRANSFER_COUNT, CHOLESKY_COUNT), jnp.float32), jnp.zeros((NW,), jnp.float32))
    (bias, exchange_sum), unused = lax.scan(advance, initial, (cholesky, slot_source, block_transfer_index, slot_multiplicity))
    bias = bias.reshape(NW, 2, TRANSFER_COUNT * CHOLESKY_COUNT)
    real_bias = bias[:, 0]
    imag_bias = bias[:, 1]
    flat_fields = fields.reshape(NW, TRANSFER_COUNT * CHOLESKY_COUNT)
    coulomb = 0.5 * lax.optimization_barrier(jnp.sum(real_bias * real_bias - imag_bias * imag_bias, axis=1))
    energy = coulomb - 0.5 * exchange_sum
    shift_real = sqrt_step * real_bias
    shift_imag = sqrt_step * imag_bias
    real_arg = lax.optimization_barrier(jnp.sum(flat_fields * shift_real - 0.5 * (shift_real * shift_real - shift_imag * shift_imag), axis=1))
    imag_arg = lax.optimization_barrier(jnp.sum(flat_fields * shift_imag - shift_real * shift_imag, axis=1))
    new_weight = weight * jnp.exp(real_arg) * jnp.maximum(jnp.cos(imag_arg), 0.0)
    mixed = jnp.sum(weight * energy) / jnp.sum(weight)
    return (bias, energy, new_weight, mixed)
```

```python
import functools

import jax
import jax.numpy as jnp
from jax import lax
from jax.experimental import pallas as pl
from jax.experimental.pallas import tpu as pltpu
from jax.sharding import PartitionSpec as P

ORBITAL_COUNT = 96
OCCUPIED_COUNT = 16
TRANSFER_COUNT = 16
SQRT_STEP = 0.05

DOUBLED = 2 * ORBITAL_COUNT
PAIR = 2 * DOUBLED
WINDOW = 256
SHIFT = PAIR - WINDOW
LANES = 128
BLOCK = 16
VMEM_LIMIT = 60 * 1024 * 1024
F32 = jnp.float32
MESH = pl.DeviceIdType.MESH


def offsets_of(devices):
    return [0, devices - 1, 1, devices // 2]


def row_of(part, occupied, walkers):
    half = (OCCUPIED_COUNT // 2) * walkers
    return part * 2 * half + (occupied % 2) * half + (occupied // 2) * walkers


def on_diagonal(count):
    return lax.broadcasted_iota(jnp.int32, (count, count), 0) == lax.broadcasted_iota(jnp.int32, (count, count), 1)


def column_of(row):
    count = row.shape[1]
    return jnp.sum(jnp.where(on_diagonal(count), jnp.broadcast_to(row, (count, count)), 0.0), axis=1, keepdims=True)


def row_from(column):
    count = column.shape[0]
    return jnp.sum(jnp.where(on_diagonal(count), jnp.broadcast_to(column, (count, count)), 0.0), axis=0, keepdims=True)


def step_kernel(
    devices,
    groups,
    source_ref,
    transfer_ref,
    multiple_ref,
    greens_hbm,
    chol_hbm,
    fields_hbm,
    weight_ref,
    bias_ref,
    energy_ref,
    new_ref,
    mixed_ref,
    greens,
    fields,
    raw,
    wide,
    chol,
    picked,
    arrived,
    dense_left,
    operand,
    product,
    tails,
    crossed,
    mine,
    theirs,
    rows_of_field,
    linear,
    summed,
    landed,
    own_sums,
    other_sums,
    own_mean,
    other_mean,
    local_sem,
    green_send,
    green_recv,
    pair_send,
    pair_recv,
    share_send,
    share_recv,
    sum_send,
    sum_recv,
    mean_send,
    mean_recv,
):
    me = lax.axis_index("pb")
    group = lax.axis_index("walk")
    slots, _, walkers, _ = mine.shape
    vectors = chol_hbm.shape[0]
    per_vector = chol_hbm.shape[1]
    kpoints = greens.shape[0] // walkers
    tiles = per_vector // slots
    pairs = OCCUPIED_COUNT // 2
    lines = devices // 2
    parity, line = lax.rem(me, 2), me // 2
    width = bias_ref.shape[2]
    offsets = offsets_of(devices)

    def pb_peer(step):
        return {"pb": lax.rem(me + step, devices)}

    def walk_peer(step):
        return {"walk": lax.rem(group + step, groups)}

    barrier = pltpu.get_barrier_semaphore()
    for step in range(1, devices):
        pl.semaphore_signal(barrier, inc=1, device_id=pb_peer(step), device_id_type=MESH)
    for step in range(1, groups):
        pl.semaphore_signal(barrier, inc=1, device_id=walk_peer(step), device_id_type=MESH)

    green_in = pltpu.make_async_copy(greens_hbm, greens, local_sem.at[0])
    green_in.start()
    chunk = -(-vectors // (4 * BLOCK)) * BLOCK
    pieces = []
    for number, first in enumerate(range(0, vectors, chunk)):
        count = min(chunk, vectors - first)
        piece = pltpu.make_async_copy(
            chol_hbm.at[pl.ds(first, count)], raw.at[pl.ds(first, count)], local_sem.at[2 + number]
        )
        piece.start()
        pieces.append((first, count, piece))
    field_in = pltpu.make_async_copy(fields_hbm, fields, local_sem.at[1])
    field_in.start()

    green_in.wait()
    lane = lax.broadcasted_iota(jnp.int32, (walkers, walkers * kpoints), 1)
    row = lax.broadcasted_iota(jnp.int32, (walkers, walkers * kpoints), 0)
    chosen = []
    for slot in range(slots):
        requester = lax.rem(me + devices - offsets[slot], devices)
        index = lax.rem(source_ref[requester * slots + slot], kpoints)
        chosen.append(jnp.where(lane == row * kpoints + index, 1.0, 0.0))
    chosen = jnp.concatenate(chosen, 0).astype(greens.dtype)
    flat = greens.shape[1]
    span = PAIR * 2
    for first in range(0, flat, span):
        rows = jnp.dot(chosen, greens[:, first : first + span], preferred_element_type=F32).astype(greens.dtype)
        arrived[0, :, first : first + span] = rows[:walkers]
        for slot in range(1, slots):
            picked[slot - 1, :, first : first + span] = rows[slot * walkers : (slot + 1) * walkers]

    pl.semaphore_wait(barrier, devices + groups - 2)

    def green_copy(slot):
        return pltpu.make_async_remote_copy(
            src_ref=picked.at[slot - 1],
            dst_ref=arrived.at[slot],
            send_sem=green_send.at[slot - 1],
            recv_sem=green_recv.at[slot - 1],
            device_id=pb_peer(devices - offsets[slot] if slot else 0),
            device_id_type=MESH,
        )

    for slot in range(1, slots):
        green_copy(slot).start()

    def split(block, carry):
        first = pl.multiple_of(block * BLOCK, BLOCK)
        for n in range(BLOCK):
            wide[n * per_vector : (n + 1) * per_vector, :] = raw[first + n].astype(F32)
        for slot in range(slots):
            for tile in range(tiles):
                part = wide[pl.ds(tile * slots + slot, BLOCK, stride=per_vector), :]
                chol[slot, pl.ds(first, BLOCK), tile * LANES : (tile + 1) * LANES] = part.astype(chol.dtype)
        return carry

    for first, count, piece in pieces:
        piece.wait()
        lax.fori_loop(first // BLOCK, -(-(first + count) // BLOCK), split, 0)
    field_in.wait()
    tails[...] = jnp.zeros_like(tails)
    linear[...] = jnp.zeros_like(linear)
    crossed[...] = jnp.zeros_like(crossed)

    pair_lane = lax.broadcasted_iota(jnp.int32, (walkers, PAIR), 1)
    is_real = lax.rem(pair_lane, DOUBLED) < ORBITAL_COUNT
    window_lane = lax.broadcasted_iota(jnp.int32, (walkers, WINDOW), 1)

    def arranged(slot, p):
        both = arrived[slot, :, PAIR * p : PAIR * (p + 1)].astype(F32)
        real = jnp.where(is_real, both, -both)
        imag = jnp.where(is_real, pltpu.roll(both, PAIR - ORBITAL_COUNT, 1), pltpu.roll(both, ORBITAL_COUNT, 1))
        return real, imag

    def pair_copy(slot):
        return pltpu.make_async_remote_copy(
            src_ref=mine.at[slot],
            dst_ref=theirs.at[slot],
            send_sem=pair_send.at[slot],
            recv_sem=pair_recv.at[slot],
            device_id={"pb": 2 * line + 1 - parity},
            device_id_type=MESH,
        )

    def traces(slot):
        for p in range(pairs):
            for part, value in enumerate(arranged(slot, p)):
                dense_left[part * walkers : (part + 1) * walkers, PAIR * p : PAIR * (p + 1)] = value.astype(
                    dense_left.dtype
                )
        trace = lax.dot_general(
            dense_left[...], chol[slot, :vectors, :], (((1,), (1,)), ((), ())), preferred_element_type=F32
        )
        trace = trace * multiple_ref[slot].astype(F32)
        transfer = transfer_ref[slot]
        for w in range(walkers):
            rows_of_field[w : w + 1, :] = fields[w, pl.ds(transfer, 1), :]
        mark = jnp.full((walkers, mine.shape[3]), transfer.astype(F32))
        for part in range(2):
            value = trace[part * walkers : (part + 1) * walkers]
            mine[slot, part] = mark
            mine[slot, part, :, :vectors] = value
            linear[part] += rows_of_field[...] * value
        pair_copy(slot).start()

    main = vectors // WINDOW * WINDOW
    rest_count = vectors - main

    def window_of(i):
        start = PAIR * (i // 2) + SHIFT * (i % 2)
        return slice(start, start + WINDOW)

    def exchange(slot):
        for p in range(pairs):
            for part, value in enumerate(arranged(slot, p)):
                low, high = value[:, :WINDOW], value[:, SHIFT:]
                even, odd = row_of(part, 2 * p, walkers), row_of(part, 2 * p + 1, walkers)
                last = WINDOW - DOUBLED
                operand[0, even : even + walkers, :] = jnp.where(window_lane < DOUBLED, low, 0.0).astype(operand.dtype)
                operand[1, even : even + walkers, :] = jnp.where(
                    window_lane >= last, pltpu.roll(low, last, 1), 0.0
                ).astype(operand.dtype)
                operand[0, odd : odd + walkers, :] = jnp.where(
                    window_lane < DOUBLED, pltpu.roll(high, DOUBLED, 1), 0.0
                ).astype(operand.dtype)
                operand[1, odd : odd + walkers, :] = jnp.where(window_lane >= last, high, 0.0).astype(operand.dtype)

        def times(which, right):
            return lax.dot_general(operand[which], right, (((1,), (1,)), ((), ())), preferred_element_type=F32)

        for i in range(OCCUPIED_COUNT):
            tails[i % 2, pl.ds(LANES * (i // 2), rest_count), :] = chol[slot, main:vectors, window_of(i)]
        for which in range(2):
            ends = times(which, tails[which])
            for p in range(pairs):
                product[2 * p + which, :, main : main + LANES] = ends[:, LANES * p : LANES * (p + 1)]

        def multiply(i):
            product[i, :, :main] = times(i % 2, chol[slot, :main, window_of(i)])

        def block(i, j, part):
            return product[i, pl.ds(row_of(part, j, walkers), walkers), :]

        zero = jnp.zeros((walkers, main + LANES), F32)
        off = [zero, zero]
        own = [zero, zero]
        multiply(0)
        for i in range(OCCUPIED_COUNT):
            if i + 1 < OCCUPIED_COUNT:
                multiply(i + 1)
            for part in range(2):
                here = block(i, i, part)
                own[part] = own[part] + here * here
                for j in range(i):
                    off[part] = off[part] + block(i, j, part) * block(j, i, part)
        crossed[...] += multiple_ref[slot].astype(F32) * ((own[0] - own[1]) + 2.0 * (off[0] - off[1]))[:, :vectors]

    def share_copy(step):
        owner = 2 * lax.rem(line + step, lines) + parity
        return pltpu.make_async_remote_copy(
            src_ref=summed.at[step],
            dst_ref=landed.at[step - 1],
            send_sem=share_send.at[step - 1],
            recv_sem=share_recv.at[step - 1],
            device_id={"pb": owner},
            device_id_type=MESH,
        )

    def terms_of(transfer, part):
        value = jnp.zeros((walkers, vectors), F32)
        for held in (mine, theirs):
            for slot in range(slots):
                here = held[slot, part]
                value = value + jnp.where(here[:, vectors : vectors + 1] == transfer, here[:, :vectors], 0.0)
        return value

    def share_of(step):
        owner = 2 * lax.rem(line + step, lines) + parity
        for part in range(2):
            if width % vectors == 0:
                each = width // vectors
                for index in range(each):
                    value = terms_of((owner * each + index).astype(F32), part)
                    summed[step, part, :, index * vectors : (index + 1) * vectors] = value
            else:
                per = vectors // width
                value = terms_of((owner // per).astype(F32), part)
                piece = lax.rem(owner, per)
                taken = value[:, :width]
                for index in range(1, per):
                    taken = jnp.where(piece == index, value[:, index * width : (index + 1) * width], taken)
                summed[step, part] = taken

    order = [lines // 2] + [step for step in range(1, lines) if step != lines // 2]

    def round_of(slot, carry):
        @pl.when(slot == 0)
        def _():
            traces(0)

        @pl.when(slot == 1)
        def _():
            for other in range(1, slots):
                green_copy(other).wait_recv()

            def one(other, inner):
                traces(other)
                return inner

            lax.fori_loop(1, slots, one, 0)

        exchange(slot)

        @pl.when(slot == 1)
        def _():
            for held in range(slots):
                pair_copy(held).wait_recv()
            for step in order:
                share_of(step)
                share_copy(step).start()
            share_of(0)

        return carry

    lax.fori_loop(0, slots, round_of, 0)

    weight = column_of(weight_ref[...])
    real = summed[0, 0]
    imag = summed[0, 1]
    for step in range(1, lines):
        share_copy(step).wait_recv()
        real = real + landed[step - 1, 0]
        imag = imag + landed[step - 1, 1]
    bias_ref[:, 0, :] = real
    bias_ref[:, 1, :] = imag
    coulomb = jnp.sum(real * real - imag * imag, axis=1, keepdims=True)
    mixed_part = jnp.sum(real * imag, axis=1, keepdims=True)
    square = SQRT_STEP * SQRT_STEP
    real_arg = SQRT_STEP * jnp.sum(linear[0], axis=1, keepdims=True) - (0.5 * square) * coulomb
    imag_arg = SQRT_STEP * jnp.sum(linear[1], axis=1, keepdims=True) - square * mixed_part
    energy_part = 0.5 * coulomb - 0.5 * jnp.sum(crossed[...], axis=1, keepdims=True)
    lane = lax.broadcasted_iota(jnp.int32, own_sums.shape, 1)
    packed = jnp.where(lane == 0, energy_part, jnp.where(lane == 1, real_arg, jnp.where(lane == 2, imag_arg, 0.0)))
    own_sums[...] = packed

    def send_all(source, target, send_sems, recv_sems, peer, count):
        copies = []
        for step in range(1, count):
            copy = pltpu.make_async_remote_copy(
                src_ref=source,
                dst_ref=target.at[step - 1],
                send_sem=send_sems.at[step - 1],
                recv_sem=recv_sems.at[step - 1],
                device_id=peer(step),
                device_id_type=MESH,
            )
            copy.start()
            copies.append(copy)
        return copies

    sums = send_all(own_sums, other_sums, sum_send, sum_recv, pb_peer, devices)
    for copy in sums:
        copy.wait_recv()
    total = jnp.zeros_like(packed)
    for index in range(devices):
        step = lax.rem(me + devices - index, devices)
        total = total + jnp.where(step == 0, packed, other_sums[jnp.maximum(step - 1, 0)])
    energy = total[:, 0:1]
    weighted = jnp.sum(weight * energy, axis=0, keepdims=True)
    weights = jnp.sum(weight, axis=0, keepdims=True)
    lane = lax.broadcasted_iota(jnp.int32, own_mean.shape, 1)
    mean = jnp.where(lane == 0, weighted, jnp.where(lane == 1, weights, 0.0))
    own_mean[...] = mean
    means = send_all(own_mean, other_mean, mean_send, mean_recv, walk_peer, groups)
    energy_ref[...] = row_from(energy)
    new_ref[...] = row_from(weight * jnp.exp(total[:, 1:2]) * jnp.maximum(jnp.cos(total[:, 2:3]), 0.0))
    for copy in means:
        copy.wait_recv()
    total = jnp.zeros_like(mean)
    for index in range(groups):
        step = lax.rem(group + groups - index, groups)
        total = total + jnp.where(step == 0, mean, other_mean[jnp.maximum(step - 1, 0)])
    mixed_ref[...] = total[0:1, 0:1] / total[0:1, 1:2]
    for slot in range(1, slots):
        green_copy(slot).wait_send()
    for slot in range(slots):
        pair_copy(slot).wait_send()
    for step in range(1, lines):
        share_copy(step).wait_send()
    for copy in sums + means:
        copy.wait_send()


def local(greens, cholesky, slot_source, block_transfer_index, slot_multiplicity, fields, weight):
    devices = lax.axis_size("pb")
    groups = lax.axis_size("walk")
    walkers, kpoints, flat = greens.shape
    slots, vectors, _ = cholesky.shape
    width = TRANSFER_COUNT * vectors // devices
    lines = devices // 2
    tiles = flat // LANES
    padded = -(-vectors // BLOCK) * BLOCK
    lanes = (vectors // LANES + 1) * LANES
    main = vectors // WINDOW * WINDOW
    rows = 2 * OCCUPIED_COUNT * walkers
    half = greens.dtype
    vmem = pl.BlockSpec(memory_space=pltpu.VMEM)
    smem = pl.BlockSpec(memory_space=pltpu.SMEM)
    hbm = pl.BlockSpec(memory_space=pl.ANY)
    dma = pltpu.SemaphoreType.DMA

    by_vector = (
        cholesky.reshape(slots, vectors, tiles, LANES).transpose(1, 2, 0, 3).reshape(vectors, tiles * slots, LANES)
    )
    bias, energy, new_weight, mixed = pl.pallas_call(
        functools.partial(step_kernel, devices, groups),
        out_shape=(
            jax.ShapeDtypeStruct((walkers, 2, width), F32),
            jax.ShapeDtypeStruct((1, walkers), F32),
            jax.ShapeDtypeStruct((1, walkers), F32),
            jax.ShapeDtypeStruct((1, 1), F32),
        ),
        in_specs=[smem, smem, smem, hbm, hbm, hbm, vmem],
        out_specs=(vmem,) * 4,
        scratch_shapes=[
            pltpu.VMEM((walkers * kpoints, flat), half),
            pltpu.VMEM(fields.shape, F32),
            pltpu.VMEM((padded, tiles * slots, LANES), half),
            pltpu.VMEM((BLOCK * tiles * slots, LANES), F32),
            pltpu.VMEM((slots, padded, flat), half),
            pltpu.VMEM((slots - 1, walkers, flat), half),
            pltpu.VMEM((slots, walkers, flat), half),
            pltpu.VMEM((2 * walkers, flat), half),
            pltpu.VMEM((2, rows, WINDOW), half),
            pltpu.VMEM((OCCUPIED_COUNT, rows, main + LANES), F32),
            pltpu.VMEM((2, LANES * OCCUPIED_COUNT // 2, WINDOW), half),
            pltpu.VMEM((walkers, vectors), F32),
            pltpu.VMEM((slots, 2, walkers, lanes), F32),
            pltpu.VMEM((slots, 2, walkers, lanes), F32),
            pltpu.VMEM((walkers, vectors), F32),
            pltpu.VMEM((2, walkers, vectors), F32),
            pltpu.VMEM((lines, 2, walkers, width), F32),
            pltpu.VMEM((lines - 1, 2, walkers, width), F32),
            pltpu.VMEM((walkers, LANES), F32),
            pltpu.VMEM((devices - 1, walkers, LANES), F32),
            pltpu.VMEM((8, LANES), F32),
            pltpu.VMEM((max(groups - 1, 1), 8, LANES), F32),
            dma((8,)),
            dma((slots - 1,)),
            dma((slots - 1,)),
            dma((slots,)),
            dma((slots,)),
            dma((lines - 1,)),
            dma((lines - 1,)),
            dma((devices - 1,)),
            dma((devices - 1,)),
            dma((max(groups - 1, 1),)),
            dma((max(groups - 1, 1),)),
        ],
        compiler_params=pltpu.CompilerParams(collective_id=1, has_side_effects=True, vmem_limit_bytes=VMEM_LIMIT),
        name="step",
    )(
        slot_source,
        block_transfer_index,
        slot_multiplicity,
        greens.reshape(walkers * kpoints, flat),
        by_vector,
        fields,
        weight.reshape(1, walkers),
    )
    return bias, energy.reshape(walkers), new_weight.reshape(walkers), mixed.reshape(())


def solution(mesh):
    placed = (
        P("walk", "pb", None),
        P("pb", None, None),
        P(),
        P("pb"),
        P("pb"),
        P("walk", None, None),
        P("walk"),
    )
    return jax.shard_map(
        local,
        mesh=mesh,
        in_specs=placed,
        out_specs=(P("walk", None, "pb"), P("walk"), P("walk"), P()),
        check_vma=False,
    )
```

```python
import functools

import jax
import jax.numpy as jnp
from jax import lax
from jax.experimental import pallas as pl
from jax.experimental.pallas import tpu as pltpu
from jax.sharding import PartitionSpec as P

ORBITAL_COUNT = 96
OCCUPIED_COUNT = 16
TRANSFER_COUNT = 16
SQRT_STEP = 0.05

DOUBLED = 2 * ORBITAL_COUNT
PAIR = 2 * DOUBLED
WINDOW = 256
SHIFT = PAIR - WINDOW
LANES = 128
BLOCK = 16
PITCH_EXTRA = 4
VMEM_LIMIT = 60 * 1024 * 1024
F32 = jnp.float32
MESH = pl.DeviceIdType.MESH


def offsets_of(devices):
    return [0, devices - 1, 1, devices // 2]


def row_of(part, occupied, walkers):
    half = (OCCUPIED_COUNT // 2) * walkers
    return part * 2 * half + (occupied % 2) * half + (occupied // 2) * walkers


def on_diagonal(count):
    return lax.broadcasted_iota(jnp.int32, (count, count), 0) == lax.broadcasted_iota(jnp.int32, (count, count), 1)


def column_of(row):
    count = row.shape[1]
    return jnp.sum(jnp.where(on_diagonal(count), jnp.broadcast_to(row, (count, count)), 0.0), axis=1, keepdims=True)


def row_from(column):
    count = column.shape[0]
    return jnp.sum(jnp.where(on_diagonal(count), jnp.broadcast_to(column, (count, count)), 0.0), axis=0, keepdims=True)


def step_kernel(
    devices,
    groups,
    source_ref,
    transfer_ref,
    multiple_ref,
    greens_hbm,
    chol_hbm,
    fields_hbm,
    weight_ref,
    bias_ref,
    total_ref,
    mean_ref,
    greens,
    fields,
    raw,
    wide,
    chol,
    picked,
    arrived,
    dense_left,
    operand,
    product,
    tails,
    crossed,
    mine,
    theirs,
    rows_of_field,
    linear,
    summed,
    landed,
    own_sums,
    other_sums,
    own_mean,
    other_mean,
    local_sem,
    green_send,
    green_recv,
    pair_send,
    pair_recv,
    share_send,
    share_recv,
    sum_send,
    sum_recv,
    mean_send,
    mean_recv,
):
    me = lax.axis_index("pb")
    group = lax.axis_index("walk")
    slots, _, walkers, _ = mine.shape
    vectors = chol_hbm.shape[0]
    per_vector = chol_hbm.shape[1]
    kpoints = greens.shape[0] // walkers
    tiles = per_vector // slots
    pitch = wide.shape[0] // BLOCK
    pairs = OCCUPIED_COUNT // 2
    lines = devices // 2
    parity, line = lax.rem(me, 2), me // 2
    width = bias_ref.shape[2]
    offsets = offsets_of(devices)

    def pb_peer(step):
        return {"pb": lax.rem(me + step, devices)}

    def walk_peer(step):
        return {"walk": lax.rem(group + step, groups)}

    barrier = pltpu.get_barrier_semaphore()
    for step in range(1, devices):
        pl.semaphore_signal(barrier, inc=1, device_id=pb_peer(step), device_id_type=MESH)
    for step in range(1, groups):
        pl.semaphore_signal(barrier, inc=1, device_id=walk_peer(step), device_id_type=MESH)

    green_in = pltpu.make_async_copy(greens_hbm, greens, local_sem.at[0])
    green_in.start()
    chunk = -(-vectors // (4 * BLOCK)) * BLOCK
    pieces = []
    for number, first in enumerate(range(0, vectors, chunk)):
        count = min(chunk, vectors - first)
        piece = pltpu.make_async_copy(
            chol_hbm.at[pl.ds(first, count)], raw.at[pl.ds(first, count)], local_sem.at[2 + number]
        )
        piece.start()
        pieces.append((first, count, piece))
    field_in = pltpu.make_async_copy(fields_hbm, fields, local_sem.at[1])
    field_in.start()

    green_in.wait()
    lane = lax.broadcasted_iota(jnp.int32, (walkers, walkers * kpoints), 1)
    row = lax.broadcasted_iota(jnp.int32, (walkers, walkers * kpoints), 0)
    chosen = []
    for slot in range(slots):
        requester = lax.rem(me + devices - offsets[slot], devices)
        index = lax.rem(source_ref[requester * slots + slot], kpoints)
        chosen.append(jnp.where(lane == row * kpoints + index, 1.0, 0.0))
    chosen = jnp.concatenate(chosen, 0).astype(greens.dtype)
    flat = greens.shape[1]
    span = PAIR * 2
    for first in range(0, flat, span):
        rows = jnp.dot(chosen, greens[:, first : first + span], preferred_element_type=F32).astype(greens.dtype)
        arrived[0, :, first : first + span] = rows[:walkers]
        for slot in range(1, slots):
            picked[slot - 1, :, first : first + span] = rows[slot * walkers : (slot + 1) * walkers]

    pl.semaphore_wait(barrier, devices + groups - 2)

    def green_copy(slot):
        return pltpu.make_async_remote_copy(
            src_ref=picked.at[slot - 1],
            dst_ref=arrived.at[slot],
            send_sem=green_send.at[slot - 1],
            recv_sem=green_recv.at[slot - 1],
            device_id=pb_peer(devices - offsets[slot] if slot else 0),
            device_id_type=MESH,
        )

    for slot in range(1, slots):
        green_copy(slot).start()

    def split(block, carry):
        first = pl.multiple_of(block * BLOCK, BLOCK)
        for n in range(BLOCK):
            wide[n * pitch : n * pitch + per_vector, :] = raw[first + n].astype(F32)
        for slot in range(slots):
            for tile in range(tiles):
                part = wide[pl.ds(tile * slots + slot, BLOCK, stride=pitch), :]
                chol[slot, pl.ds(first, BLOCK), tile * LANES : (tile + 1) * LANES] = part.astype(chol.dtype)
        return carry

    for first, count, piece in pieces:
        piece.wait()
        lax.fori_loop(first // BLOCK, -(-(first + count) // BLOCK), split, 0)
    field_in.wait()
    tails[...] = jnp.zeros_like(tails)
    linear[...] = jnp.zeros_like(linear)
    crossed[...] = jnp.zeros_like(crossed)

    pair_lane = lax.broadcasted_iota(jnp.int32, (walkers, PAIR), 1)
    is_real = lax.rem(pair_lane, DOUBLED) < ORBITAL_COUNT
    window_lane = lax.broadcasted_iota(jnp.int32, (walkers, WINDOW), 1)

    def arranged(slot, p):
        both = arrived[slot, :, PAIR * p : PAIR * (p + 1)].astype(F32)
        real = jnp.where(is_real, both, -both)
        imag = jnp.where(is_real, pltpu.roll(both, PAIR - ORBITAL_COUNT, 1), pltpu.roll(both, ORBITAL_COUNT, 1))
        return real, imag

    def pair_copy(slot):
        return pltpu.make_async_remote_copy(
            src_ref=mine.at[slot],
            dst_ref=theirs.at[slot],
            send_sem=pair_send.at[slot],
            recv_sem=pair_recv.at[slot],
            device_id={"pb": 2 * line + 1 - parity},
            device_id_type=MESH,
        )

    def traces(slot):
        for p in range(pairs):
            for part, value in enumerate(arranged(slot, p)):
                dense_left[part * walkers : (part + 1) * walkers, PAIR * p : PAIR * (p + 1)] = value.astype(
                    dense_left.dtype
                )
        trace = lax.dot_general(
            dense_left[...], chol[slot, :vectors, :], (((1,), (1,)), ((), ())), preferred_element_type=F32
        )
        trace = trace * multiple_ref[slot].astype(F32)
        transfer = transfer_ref[slot]
        for w in range(walkers):
            rows_of_field[w : w + 1, :] = fields[w, pl.ds(transfer, 1), :]
        mark = jnp.full((walkers, mine.shape[3]), transfer.astype(F32))
        for part in range(2):
            value = trace[part * walkers : (part + 1) * walkers]
            mine[slot, part] = mark
            mine[slot, part, :, :vectors] = value
            linear[part] += rows_of_field[...] * value
        pair_copy(slot).start()

    main = vectors // WINDOW * WINDOW
    rest_count = vectors - main

    def window_of(i):
        start = PAIR * (i // 2) + SHIFT * (i % 2)
        return slice(start, start + WINDOW)

    def exchange(slot):
        for p in range(pairs):
            for part, value in enumerate(arranged(slot, p)):
                low, high = value[:, :WINDOW], value[:, SHIFT:]
                even, odd = row_of(part, 2 * p, walkers), row_of(part, 2 * p + 1, walkers)
                last = WINDOW - DOUBLED
                operand[0, even : even + walkers, :] = jnp.where(window_lane < DOUBLED, low, 0.0).astype(operand.dtype)
                operand[1, even : even + walkers, :] = jnp.where(
                    window_lane >= last, pltpu.roll(low, last, 1), 0.0
                ).astype(operand.dtype)
                operand[0, odd : odd + walkers, :] = jnp.where(
                    window_lane < DOUBLED, pltpu.roll(high, DOUBLED, 1), 0.0
                ).astype(operand.dtype)
                operand[1, odd : odd + walkers, :] = jnp.where(window_lane >= last, high, 0.0).astype(operand.dtype)

        def times(which, right):
            return lax.dot_general(operand[which], right, (((1,), (1,)), ((), ())), preferred_element_type=F32)

        for i in range(OCCUPIED_COUNT):
            tails[i % 2, pl.ds(LANES * (i // 2), rest_count), :] = chol[slot, main:vectors, window_of(i)]
        for which in range(2):
            ends = times(which, tails[which])
            for p in range(pairs):
                product[2 * p + which, :, main : main + LANES] = ends[:, LANES * p : LANES * (p + 1)]

        def multiply(i):
            product[i, :, :main] = times(i % 2, chol[slot, :main, window_of(i)])

        def block(i, j, part):
            return product[i, pl.ds(row_of(part, j, walkers), walkers), :]

        zero = jnp.zeros((walkers, main + LANES), F32)
        off = [zero, zero]
        own = [zero, zero]
        multiply(0)
        for i in range(OCCUPIED_COUNT):
            if i + 1 < OCCUPIED_COUNT:
                multiply(i + 1)
            for part in range(2):
                here = block(i, i, part)
                own[part] = own[part] + here * here
                for j in range(i):
                    off[part] = off[part] + block(i, j, part) * block(j, i, part)
        crossed[...] += multiple_ref[slot].astype(F32) * ((own[0] - own[1]) + 2.0 * (off[0] - off[1]))[:, :vectors]

    def share_copy(step):
        owner = 2 * lax.rem(line + step, lines) + parity
        return pltpu.make_async_remote_copy(
            src_ref=summed.at[step],
            dst_ref=landed.at[step - 1],
            send_sem=share_send.at[step - 1],
            recv_sem=share_recv.at[step - 1],
            device_id={"pb": owner},
            device_id_type=MESH,
        )

    def terms_of(transfer, part):
        value = jnp.zeros((walkers, vectors), F32)
        for held in (mine, theirs):
            for slot in range(slots):
                here = held[slot, part]
                value = value + jnp.where(here[:, vectors : vectors + 1] == transfer, here[:, :vectors], 0.0)
        return value

    def share_of(step):
        owner = 2 * lax.rem(line + step, lines) + parity
        for part in range(2):
            if width % vectors == 0:
                each = width // vectors
                for index in range(each):
                    value = terms_of((owner * each + index).astype(F32), part)
                    summed[step, part, :, index * vectors : (index + 1) * vectors] = value
            else:
                per = vectors // width
                value = terms_of((owner // per).astype(F32), part)
                piece = lax.rem(owner, per)
                taken = value[:, :width]
                for index in range(1, per):
                    taken = jnp.where(piece == index, value[:, index * width : (index + 1) * width], taken)
                summed[step, part] = taken

    order = [lines // 2] + [step for step in range(1, lines) if step != lines // 2]

    def round_of(slot, carry):
        @pl.when(slot == 0)
        def _():
            traces(0)

        @pl.when(slot == 1)
        def _():
            for other in range(1, slots):
                green_copy(other).wait_recv()

            def one(other, inner):
                traces(other)
                return inner

            lax.fori_loop(1, slots, one, 0)

        exchange(slot)

        @pl.when(slot == 1)
        def _():
            for held in range(slots):
                pair_copy(held).wait_recv()
            for step in order:
                share_of(step)
                share_copy(step).start()
            share_of(0)

        return carry

    lax.fori_loop(0, slots, round_of, 0)

    weight = column_of(weight_ref[...])
    real = summed[0, 0]
    imag = summed[0, 1]
    for step in range(1, lines):
        share_copy(step).wait_recv()
        real = real + landed[step - 1, 0]
        imag = imag + landed[step - 1, 1]
    bias_ref[0] = real
    bias_ref[1] = imag
    coulomb = jnp.sum(real * real - imag * imag, axis=1, keepdims=True)
    mixed_part = jnp.sum(real * imag, axis=1, keepdims=True)
    square = SQRT_STEP * SQRT_STEP
    real_arg = SQRT_STEP * jnp.sum(linear[0], axis=1, keepdims=True) - (0.5 * square) * coulomb
    imag_arg = SQRT_STEP * jnp.sum(linear[1], axis=1, keepdims=True) - square * mixed_part
    energy_part = 0.5 * coulomb - 0.5 * jnp.sum(crossed[...], axis=1, keepdims=True)
    lane = lax.broadcasted_iota(jnp.int32, own_sums.shape, 1)
    packed = jnp.where(lane == 0, energy_part, jnp.where(lane == 1, real_arg, jnp.where(lane == 2, imag_arg, 0.0)))
    own_sums[...] = packed

    def send_all(source, target, send_sems, recv_sems, peer, count):
        copies = []
        for step in range(1, count):
            copy = pltpu.make_async_remote_copy(
                src_ref=source,
                dst_ref=target.at[step - 1],
                send_sem=send_sems.at[step - 1],
                recv_sem=recv_sems.at[step - 1],
                device_id=peer(step),
                device_id_type=MESH,
            )
            copy.start()
            copies.append(copy)
        return copies

    sums = send_all(own_sums, other_sums, sum_send, sum_recv, pb_peer, devices)
    for copy in sums:
        copy.wait_recv()
    total = jnp.zeros_like(packed)
    for index in range(devices):
        step = lax.rem(me + devices - index, devices)
        total = total + jnp.where(step == 0, packed, other_sums[jnp.maximum(step - 1, 0)])
    total_ref[...] = total
    energy = total[:, 0:1]
    weighted = jnp.sum(weight * energy, axis=0, keepdims=True)
    weights = jnp.sum(weight, axis=0, keepdims=True)
    lane = lax.broadcasted_iota(jnp.int32, own_mean.shape, 1)
    mean = jnp.where(lane == 0, weighted, jnp.where(lane == 1, weights, 0.0))
    own_mean[...] = mean
    means = send_all(own_mean, other_mean, mean_send, mean_recv, walk_peer, groups)
    for copy in means:
        copy.wait_recv()
    total = jnp.zeros_like(mean)
    for index in range(groups):
        step = lax.rem(group + groups - index, groups)
        total = total + jnp.where(step == 0, mean, other_mean[jnp.maximum(step - 1, 0)])
    mean_ref[...] = total
    for slot in range(1, slots):
        green_copy(slot).wait_send()
    for slot in range(slots):
        pair_copy(slot).wait_send()
    for step in range(1, lines):
        share_copy(step).wait_send()
    for copy in sums + means:
        copy.wait_send()


def finish_kernel(sums_ref, total_ref, mean_ref, weight_ref, bias_ref, energy_ref, new_ref, mixed_ref):
    bias_ref[:, 0, :] = sums_ref[0]
    bias_ref[:, 1, :] = sums_ref[1]
    total = total_ref[...]
    weight = column_of(weight_ref[...])
    energy_ref[...] = row_from(total[:, 0:1])
    new_ref[...] = row_from(weight * jnp.exp(total[:, 1:2]) * jnp.maximum(jnp.cos(total[:, 2:3]), 0.0))
    mean = mean_ref[:1, :]
    mixed_ref[...] = mean[:, 0:1] / mean[:, 1:2]


def local(greens, cholesky, slot_source, block_transfer_index, slot_multiplicity, fields, weight):
    devices = lax.axis_size("pb")
    groups = lax.axis_size("walk")
    walkers, kpoints, flat = greens.shape
    slots, vectors, _ = cholesky.shape
    width = TRANSFER_COUNT * vectors // devices
    lines = devices // 2
    tiles = flat // LANES
    padded = -(-vectors // BLOCK) * BLOCK
    lanes = (vectors // LANES + 1) * LANES
    main = vectors // WINDOW * WINDOW
    rows = 2 * OCCUPIED_COUNT * walkers
    half = greens.dtype
    vmem = pl.BlockSpec(memory_space=pltpu.VMEM)
    smem = pl.BlockSpec(memory_space=pltpu.SMEM)
    hbm = pl.BlockSpec(memory_space=pl.ANY)
    dma = pltpu.SemaphoreType.DMA

    by_vector = (
        cholesky.reshape(slots, vectors, tiles, LANES).transpose(1, 2, 0, 3).reshape(vectors, tiles * slots, LANES)
    )
    sums, total, mean = pl.pallas_call(
        functools.partial(step_kernel, devices, groups),
        out_shape=(
            jax.ShapeDtypeStruct((2, walkers, width), F32),
            jax.ShapeDtypeStruct((walkers, LANES), F32),
            jax.ShapeDtypeStruct((8, LANES), F32),
        ),
        in_specs=[smem, smem, smem, hbm, hbm, hbm, vmem],
        out_specs=(vmem,) * 3,
        scratch_shapes=[
            pltpu.VMEM((walkers * kpoints, flat), half),
            pltpu.VMEM(fields.shape, F32),
            pltpu.VMEM((padded, tiles * slots, LANES), half),
            pltpu.VMEM((BLOCK * (tiles * slots + PITCH_EXTRA), LANES), F32),
            pltpu.VMEM((slots, padded, flat), half),
            pltpu.VMEM((slots - 1, walkers, flat), half),
            pltpu.VMEM((slots, walkers, flat), half),
            pltpu.VMEM((2 * walkers, flat), half),
            pltpu.VMEM((2, rows, WINDOW), half),
            pltpu.VMEM((OCCUPIED_COUNT, rows, main + LANES), F32),
            pltpu.VMEM((2, LANES * OCCUPIED_COUNT // 2, WINDOW), half),
            pltpu.VMEM((walkers, vectors), F32),
            pltpu.VMEM((slots, 2, walkers, lanes), F32),
            pltpu.VMEM((slots, 2, walkers, lanes), F32),
            pltpu.VMEM((walkers, vectors), F32),
            pltpu.VMEM((2, walkers, vectors), F32),
            pltpu.VMEM((lines, 2, walkers, width), F32),
            pltpu.VMEM((lines - 1, 2, walkers, width), F32),
            pltpu.VMEM((walkers, LANES), F32),
            pltpu.VMEM((devices - 1, walkers, LANES), F32),
            pltpu.VMEM((8, LANES), F32),
            pltpu.VMEM((max(groups - 1, 1), 8, LANES), F32),
            dma((8,)),
            dma((slots - 1,)),
            dma((slots - 1,)),
            dma((slots,)),
            dma((slots,)),
            dma((lines - 1,)),
            dma((lines - 1,)),
            dma((devices - 1,)),
            dma((devices - 1,)),
            dma((max(groups - 1, 1),)),
            dma((max(groups - 1, 1),)),
        ],
        compiler_params=pltpu.CompilerParams(collective_id=1, has_side_effects=True, vmem_limit_bytes=VMEM_LIMIT),
        name="step",
    )(
        slot_source,
        block_transfer_index,
        slot_multiplicity,
        greens.reshape(walkers * kpoints, flat),
        by_vector,
        fields,
        weight.reshape(1, walkers),
    )
    bias, energy, new_weight, mixed = pl.pallas_call(
        finish_kernel,
        out_shape=(
            jax.ShapeDtypeStruct((walkers, 2, width), F32),
            jax.ShapeDtypeStruct((1, walkers), F32),
            jax.ShapeDtypeStruct((1, walkers), F32),
            jax.ShapeDtypeStruct((1, 1), F32),
        ),
        in_specs=[vmem] * 4,
        out_specs=(vmem,) * 4,
        name="finish",
    )(sums, total, mean, weight.reshape(1, walkers))
    return bias, energy.reshape(walkers), new_weight.reshape(walkers), mixed.reshape(())


def solution(mesh):
    placed = (
        P("walk", "pb", None),
        P("pb", None, None),
        P(),
        P("pb"),
        P("pb"),
        P("walk", None, None),
        P("walk"),
    )
    return jax.shard_map(
        local,
        mesh=mesh,
        in_specs=placed,
        out_specs=(P("walk", None, "pb"), P("walk"), P("walk"), P()),
        check_vma=False,
    )
```

```python
import functools

import jax
import jax.numpy as jnp
from jax import lax
from jax.experimental import pallas as pl
from jax.experimental.pallas import tpu as pltpu
from jax.sharding import PartitionSpec as P

ORBITAL_COUNT = 96
OCCUPIED_COUNT = 16
TRANSFER_COUNT = 16
SQRT_STEP = 0.05

DOUBLED = 2 * ORBITAL_COUNT
PAIR = 2 * DOUBLED
WINDOW = 256
SHIFT = PAIR - WINDOW
LANES = 128
BLOCK = 16
PITCH_EXTRA = 4
VMEM_LIMIT = 60 * 1024 * 1024
F32 = jnp.float32
MESH = pl.DeviceIdType.MESH


def offsets_of(devices):
    return [0, devices - 1, 1, devices // 2]


def row_of(part, occupied, walkers):
    half = (OCCUPIED_COUNT // 2) * walkers
    return part * 2 * half + (occupied % 2) * half + (occupied // 2) * walkers


def on_diagonal(count):
    return lax.broadcasted_iota(jnp.int32, (count, count), 0) == lax.broadcasted_iota(jnp.int32, (count, count), 1)


def column_of(row):
    count = row.shape[1]
    return jnp.sum(jnp.where(on_diagonal(count), jnp.broadcast_to(row, (count, count)), 0.0), axis=1, keepdims=True)


def step_kernel(
    devices,
    groups,
    source_ref,
    transfer_ref,
    multiple_ref,
    greens_hbm,
    chol_hbm,
    fields_hbm,
    weight_ref,
    bias_ref,
    total_ref,
    greens,
    fields,
    raw,
    wide,
    chol,
    picked,
    arrived,
    dense_left,
    operand,
    product,
    tails,
    crossed,
    mine,
    theirs,
    rows_of_field,
    linear,
    summed,
    landed,
    packets,
    local_sem,
    green_send,
    green_recv,
    pair_send,
    pair_recv,
    share_send,
    share_recv,
    sum_send,
    sum_recv,
):
    me = lax.axis_index("pb")
    group = lax.axis_index("walk")
    slots, _, walkers, _ = mine.shape
    vectors = chol_hbm.shape[0]
    per_vector = chol_hbm.shape[1]
    kpoints = greens.shape[0] // walkers
    tiles = per_vector // slots
    pitch = wide.shape[0] // BLOCK
    pairs = OCCUPIED_COUNT // 2
    lines = devices // 2
    parity, line = lax.rem(me, 2), me // 2
    width = bias_ref.shape[2]
    offsets = offsets_of(devices)

    def pb_peer(step):
        return {"pb": lax.rem(me + step, devices)}

    everyone = devices * groups

    def peer_of(step):
        return {"walk": lax.rem(group + step // devices, groups), "pb": lax.rem(me + lax.rem(step, devices), devices)}

    def sender_of(step):
        walk = lax.rem(group + groups - step // devices, groups)
        return walk * devices + lax.rem(me + devices - lax.rem(step, devices), devices)

    barrier = pltpu.get_barrier_semaphore()

    def greet(step, carry):
        pl.semaphore_signal(barrier, inc=1, device_id=peer_of(step), device_id_type=MESH)
        return carry

    lax.fori_loop(1, everyone, greet, 0)

    green_in = pltpu.make_async_copy(greens_hbm, greens, local_sem.at[0])
    green_in.start()
    chunk = -(-vectors // (4 * BLOCK)) * BLOCK
    pieces = []
    for number, first in enumerate(range(0, vectors, chunk)):
        count = min(chunk, vectors - first)
        piece = pltpu.make_async_copy(
            chol_hbm.at[pl.ds(first, count)], raw.at[pl.ds(first, count)], local_sem.at[2 + number]
        )
        piece.start()
        pieces.append((first, count, piece))
    field_in = pltpu.make_async_copy(fields_hbm, fields, local_sem.at[1])
    field_in.start()

    green_in.wait()
    lane = lax.broadcasted_iota(jnp.int32, (walkers, walkers * kpoints), 1)
    row = lax.broadcasted_iota(jnp.int32, (walkers, walkers * kpoints), 0)
    chosen = []
    for slot in range(slots):
        requester = lax.rem(me + devices - offsets[slot], devices)
        index = lax.rem(source_ref[requester * slots + slot], kpoints)
        chosen.append(jnp.where(lane == row * kpoints + index, 1.0, 0.0))
    chosen = jnp.concatenate(chosen, 0).astype(greens.dtype)
    flat = greens.shape[1]
    span = PAIR * 2
    for first in range(0, flat, span):
        rows = jnp.dot(chosen, greens[:, first : first + span], preferred_element_type=F32).astype(greens.dtype)
        arrived[0, :, first : first + span] = rows[:walkers]
        for slot in range(1, slots):
            picked[slot - 1, :, first : first + span] = rows[slot * walkers : (slot + 1) * walkers]

    pl.semaphore_wait(barrier, everyone - 1)

    def green_copy(slot):
        return pltpu.make_async_remote_copy(
            src_ref=picked.at[slot - 1],
            dst_ref=arrived.at[slot],
            send_sem=green_send.at[slot - 1],
            recv_sem=green_recv.at[slot - 1],
            device_id=pb_peer(devices - offsets[slot] if slot else 0),
            device_id_type=MESH,
        )

    for slot in range(1, slots):
        green_copy(slot).start()

    def split(block, carry):
        first = pl.multiple_of(block * BLOCK, BLOCK)
        for n in range(BLOCK):
            wide[n * pitch : n * pitch + per_vector, :] = raw[first + n].astype(F32)
        for slot in range(slots):
            for tile in range(tiles):
                part = wide[pl.ds(tile * slots + slot, BLOCK, stride=pitch), :]
                chol[slot, pl.ds(first, BLOCK), tile * LANES : (tile + 1) * LANES] = part.astype(chol.dtype)
        return carry

    for first, count, piece in pieces:
        piece.wait()
        lax.fori_loop(first // BLOCK, -(-(first + count) // BLOCK), split, 0)
    field_in.wait()
    tails[...] = jnp.zeros_like(tails)
    linear[...] = jnp.zeros_like(linear)
    crossed[...] = jnp.zeros_like(crossed)

    pair_lane = lax.broadcasted_iota(jnp.int32, (walkers, PAIR), 1)
    is_real = lax.rem(pair_lane, DOUBLED) < ORBITAL_COUNT
    window_lane = lax.broadcasted_iota(jnp.int32, (walkers, WINDOW), 1)

    def arranged(slot, p):
        both = arrived[slot, :, PAIR * p : PAIR * (p + 1)].astype(F32)
        real = jnp.where(is_real, both, -both)
        imag = jnp.where(is_real, pltpu.roll(both, PAIR - ORBITAL_COUNT, 1), pltpu.roll(both, ORBITAL_COUNT, 1))
        return real, imag

    def pair_copy(slot):
        return pltpu.make_async_remote_copy(
            src_ref=mine.at[slot],
            dst_ref=theirs.at[slot],
            send_sem=pair_send.at[slot],
            recv_sem=pair_recv.at[slot],
            device_id={"pb": 2 * line + 1 - parity},
            device_id_type=MESH,
        )

    def traces(slot):
        for p in range(pairs):
            for part, value in enumerate(arranged(slot, p)):
                dense_left[part * walkers : (part + 1) * walkers, PAIR * p : PAIR * (p + 1)] = value.astype(
                    dense_left.dtype
                )
        trace = lax.dot_general(
            dense_left[...], chol[slot, :vectors, :], (((1,), (1,)), ((), ())), preferred_element_type=F32
        )
        trace = trace * multiple_ref[slot].astype(F32)
        transfer = transfer_ref[slot]
        for w in range(walkers):
            rows_of_field[w : w + 1, :] = fields[w, pl.ds(transfer, 1), :]
        mark = jnp.full((walkers, mine.shape[3]), transfer.astype(F32))
        for part in range(2):
            value = trace[part * walkers : (part + 1) * walkers]
            mine[slot, part] = mark
            mine[slot, part, :, :vectors] = value
            linear[part] += rows_of_field[...] * value
        pair_copy(slot).start()

    main = vectors // WINDOW * WINDOW
    rest_count = vectors - main

    def window_of(i):
        start = PAIR * (i // 2) + SHIFT * (i % 2)
        return slice(start, start + WINDOW)

    def exchange(slot):
        for p in range(pairs):
            for part, value in enumerate(arranged(slot, p)):
                low, high = value[:, :WINDOW], value[:, SHIFT:]
                even, odd = row_of(part, 2 * p, walkers), row_of(part, 2 * p + 1, walkers)
                last = WINDOW - DOUBLED
                operand[0, even : even + walkers, :] = jnp.where(window_lane < DOUBLED, low, 0.0).astype(operand.dtype)
                operand[1, even : even + walkers, :] = jnp.where(
                    window_lane >= last, pltpu.roll(low, last, 1), 0.0
                ).astype(operand.dtype)
                operand[0, odd : odd + walkers, :] = jnp.where(
                    window_lane < DOUBLED, pltpu.roll(high, DOUBLED, 1), 0.0
                ).astype(operand.dtype)
                operand[1, odd : odd + walkers, :] = jnp.where(window_lane >= last, high, 0.0).astype(operand.dtype)

        def times(which, right):
            return lax.dot_general(operand[which], right, (((1,), (1,)), ((), ())), preferred_element_type=F32)

        for i in range(OCCUPIED_COUNT):
            tails[i % 2, pl.ds(LANES * (i // 2), rest_count), :] = chol[slot, main:vectors, window_of(i)]
        for which in range(2):
            ends = times(which, tails[which])
            for p in range(pairs):
                product[2 * p + which, :, main : main + LANES] = ends[:, LANES * p : LANES * (p + 1)]

        def multiply(i):
            product[i, :, :main] = times(i % 2, chol[slot, :main, window_of(i)])

        def block(i, j, part):
            return product[i, pl.ds(row_of(part, j, walkers), walkers), :]

        zero = jnp.zeros((walkers, main + LANES), F32)
        off = [zero, zero]
        own = [zero, zero]
        multiply(0)
        for i in range(OCCUPIED_COUNT):
            if i + 1 < OCCUPIED_COUNT:
                multiply(i + 1)
            for part in range(2):
                here = block(i, i, part)
                own[part] = own[part] + here * here
                for j in range(i):
                    off[part] = off[part] + block(i, j, part) * block(j, i, part)
        crossed[...] += multiple_ref[slot].astype(F32) * ((own[0] - own[1]) + 2.0 * (off[0] - off[1]))[:, :vectors]

    def share_copy(step):
        owner = 2 * lax.rem(line + step, lines) + parity
        return pltpu.make_async_remote_copy(
            src_ref=summed.at[step],
            dst_ref=landed.at[step - 1],
            send_sem=share_send.at[step - 1],
            recv_sem=share_recv.at[step - 1],
            device_id={"pb": owner},
            device_id_type=MESH,
        )

    def terms_of(transfer, part):
        value = jnp.zeros((walkers, vectors), F32)
        for held in (mine, theirs):
            for slot in range(slots):
                here = held[slot, part]
                value = value + jnp.where(here[:, vectors : vectors + 1] == transfer, here[:, :vectors], 0.0)
        return value

    def share_of(step):
        owner = 2 * lax.rem(line + step, lines) + parity
        for part in range(2):
            if width % vectors == 0:
                each = width // vectors
                for index in range(each):
                    value = terms_of((owner * each + index).astype(F32), part)
                    summed[step, part, :, index * vectors : (index + 1) * vectors] = value
            else:
                per = vectors // width
                value = terms_of((owner // per).astype(F32), part)
                piece = lax.rem(owner, per)
                taken = value[:, :width]
                for index in range(1, per):
                    taken = jnp.where(piece == index, value[:, index * width : (index + 1) * width], taken)
                summed[step, part] = taken

    order = [lines // 2] + [step for step in range(1, lines) if step != lines // 2]

    def round_of(slot, carry):
        @pl.when(slot == 0)
        def _():
            traces(0)

        @pl.when(slot == 1)
        def _():
            def one(other, inner):
                pltpu.make_async_remote_copy(
                    src_ref=picked.at[other - 1],
                    dst_ref=arrived.at[other],
                    send_sem=green_send.at[other - 1],
                    recv_sem=green_recv.at[other - 1],
                    device_id={"pb": 2 * line + 1 - parity},
                    device_id_type=MESH,
                ).wait_recv()
                traces(other)
                return inner

            lax.fori_loop(1, slots, one, 0)

        exchange(slot)

        @pl.when(slot == 1)
        def _():
            for held in range(slots):
                pair_copy(held).wait_recv()
            for step in order:
                share_of(step)
                share_copy(step).start()
            share_of(0)

        return carry

    lax.fori_loop(0, slots, round_of, 0)

    weight = column_of(weight_ref[...])
    real = summed[0, 0]
    imag = summed[0, 1]
    for step in range(1, lines):
        share_copy(step).wait_recv()
        real = real + landed[step - 1, 0]
        imag = imag + landed[step - 1, 1]
    bias_ref[0] = real
    bias_ref[1] = imag
    coulomb = jnp.sum(real * real - imag * imag, axis=1, keepdims=True)
    mixed_part = jnp.sum(real * imag, axis=1, keepdims=True)
    square = SQRT_STEP * SQRT_STEP
    real_arg = SQRT_STEP * jnp.sum(linear[0], axis=1, keepdims=True) - (0.5 * square) * coulomb
    imag_arg = SQRT_STEP * jnp.sum(linear[1], axis=1, keepdims=True) - square * mixed_part
    energy_part = 0.5 * coulomb - 0.5 * jnp.sum(crossed[...], axis=1, keepdims=True)
    shape = (walkers, LANES)
    lane = lax.broadcasted_iota(jnp.int32, shape, 1)
    row = lax.broadcasted_iota(jnp.int32, shape, 0)
    values = (energy_part, real_arg, imag_arg)
    packet = jnp.zeros(shape, F32)
    for number, value in enumerate(values):
        packet = jnp.where(lane == row + number * walkers, value, packet)
    tail = len(values) * walkers
    packet = jnp.where(lane == tail, weight * energy_part, packet)
    packet = jnp.where(lane == tail + 1, weight * (1.0 / devices), packet)
    packets[group * devices + me] = jnp.sum(packet, axis=0, keepdims=True)

    def packet_out(step):
        mine_at = group * devices + me
        return pltpu.make_async_remote_copy(
            src_ref=packets.at[mine_at],
            dst_ref=packets.at[mine_at],
            send_sem=sum_send.at[step - 1],
            recv_sem=sum_recv.at[step - 1],
            device_id=peer_of(step),
            device_id_type=MESH,
        )

    def packet_in(step):
        at = sender_of(step)
        return pltpu.make_async_remote_copy(
            src_ref=packets.at[at],
            dst_ref=packets.at[at],
            send_sem=sum_send.at[step - 1],
            recv_sem=sum_recv.at[step - 1],
            device_id=peer_of(step),
            device_id_type=MESH,
        )

    def send_packet(step, carry):
        packet_out(everyone - step).start()
        return carry

    def take_packet(step, carry):
        packet_in(step).wait_recv()
        return carry

    def packet_sent(step, carry):
        packet_out(step).wait_send()
        return carry

    lax.fori_loop(1, everyone, send_packet, 0)
    lax.fori_loop(1, everyone, take_packet, 0)
    total = jnp.zeros((1, LANES), F32)
    for index in range(devices):
        total = total + packets[group * devices + index]
    whole = jnp.zeros((1, LANES), F32)
    for index in range(everyone):
        whole = whole + packets[index]
    lane = lax.broadcasted_iota(jnp.int32, (1, LANES), 1)
    total_ref[...] = jnp.where(lane < tail, total, whole)
    lax.fori_loop(1, everyone, packet_sent, 0)
    for slot in range(1, slots):
        green_copy(slot).wait_send()
    for slot in range(slots):
        pair_copy(slot).wait_send()
    for step in range(1, lines):
        share_copy(step).wait_send()


def finish_kernel(sums_ref, total_ref, weight_ref, bias_ref, energy_ref, new_ref, mixed_ref):
    bias_ref[:, 0, :] = sums_ref[0]
    bias_ref[:, 1, :] = sums_ref[1]
    total = total_ref[...]
    weight = weight_ref[...]
    walkers = weight.shape[1]
    energy_ref[...] = total[:, :walkers]
    real, imag = total[:, walkers : 2 * walkers], total[:, 2 * walkers : 3 * walkers]
    new_ref[...] = weight * jnp.exp(real) * jnp.maximum(jnp.cos(imag), 0.0)
    tail = 3 * walkers
    mixed_ref[...] = total[:, tail : tail + 1] / total[:, tail + 1 : tail + 2]


def local(greens, cholesky, slot_source, block_transfer_index, slot_multiplicity, fields, weight):
    devices = lax.axis_size("pb")
    groups = lax.axis_size("walk")
    walkers, kpoints, flat = greens.shape
    slots, vectors, _ = cholesky.shape
    width = TRANSFER_COUNT * vectors // devices
    lines = devices // 2
    tiles = flat // LANES
    padded = -(-vectors // BLOCK) * BLOCK
    lanes = (vectors // LANES + 1) * LANES
    main = vectors // WINDOW * WINDOW
    rows = 2 * OCCUPIED_COUNT * walkers
    half = greens.dtype
    vmem = pl.BlockSpec(memory_space=pltpu.VMEM)
    smem = pl.BlockSpec(memory_space=pltpu.SMEM)
    hbm = pl.BlockSpec(memory_space=pl.ANY)
    dma = pltpu.SemaphoreType.DMA

    by_vector = (
        cholesky.reshape(slots, vectors, tiles, LANES).transpose(1, 2, 0, 3).reshape(vectors, tiles * slots, LANES)
    )
    sums, total = pl.pallas_call(
        functools.partial(step_kernel, devices, groups),
        out_shape=(
            jax.ShapeDtypeStruct((2, walkers, width), F32),
            jax.ShapeDtypeStruct((1, LANES), F32),
        ),
        in_specs=[smem, smem, smem, hbm, hbm, hbm, vmem],
        out_specs=(vmem,) * 2,
        scratch_shapes=[
            pltpu.VMEM((walkers * kpoints, flat), half),
            pltpu.VMEM(fields.shape, F32),
            pltpu.VMEM((padded, tiles * slots, LANES), half),
            pltpu.VMEM((BLOCK * (tiles * slots + PITCH_EXTRA), LANES), F32),
            pltpu.VMEM((slots, padded, flat), half),
            pltpu.VMEM((slots - 1, walkers, flat), half),
            pltpu.VMEM((slots, walkers, flat), half),
            pltpu.VMEM((2 * walkers, flat), half),
            pltpu.VMEM((2, rows, WINDOW), half),
            pltpu.VMEM((OCCUPIED_COUNT, rows, main + LANES), F32),
            pltpu.VMEM((2, LANES * OCCUPIED_COUNT // 2, WINDOW), half),
            pltpu.VMEM((walkers, vectors), F32),
            pltpu.VMEM((slots, 2, walkers, lanes), F32),
            pltpu.VMEM((slots, 2, walkers, lanes), F32),
            pltpu.VMEM((walkers, vectors), F32),
            pltpu.VMEM((2, walkers, vectors), F32),
            pltpu.VMEM((lines, 2, walkers, width), F32),
            pltpu.VMEM((lines - 1, 2, walkers, width), F32),
            pltpu.VMEM((devices * groups, 1, LANES), F32),
            dma((8,)),
            dma((slots - 1,)),
            dma((slots - 1,)),
            dma((slots,)),
            dma((slots,)),
            dma((lines - 1,)),
            dma((lines - 1,)),
            dma((devices * groups - 1,)),
            dma((devices * groups - 1,)),
        ],
        compiler_params=pltpu.CompilerParams(collective_id=1, has_side_effects=True, vmem_limit_bytes=VMEM_LIMIT),
        name="step",
    )(
        slot_source,
        block_transfer_index,
        slot_multiplicity,
        greens.reshape(walkers * kpoints, flat),
        by_vector,
        fields,
        weight.reshape(1, walkers),
    )
    bias, energy, new_weight, mixed = pl.pallas_call(
        finish_kernel,
        out_shape=(
            jax.ShapeDtypeStruct((walkers, 2, width), F32),
            jax.ShapeDtypeStruct((1, walkers), F32),
            jax.ShapeDtypeStruct((1, walkers), F32),
            jax.ShapeDtypeStruct((1, 1), F32),
        ),
        in_specs=[vmem] * 3,
        out_specs=(vmem,) * 4,
        name="finish",
    )(sums, total, weight.reshape(1, walkers))
    return bias, energy.reshape(walkers), new_weight.reshape(walkers), mixed.reshape(())


def solution(mesh):
    placed = (
        P("walk", "pb", None),
        P("pb", None, None),
        P(),
        P("pb"),
        P("pb"),
        P("walk", None, None),
        P("walk"),
    )
    return jax.shard_map(
        local,
        mesh=mesh,
        in_specs=placed,
        out_specs=(P("walk", None, "pb"), P("walk"), P("walk"), P()),
        check_vma=False,
    )
```

```python
import functools

import jax
import jax.numpy as jnp
from jax import lax
from jax.experimental import pallas as pl
from jax.experimental.pallas import tpu as pltpu
from jax.sharding import PartitionSpec as P

ORBITAL_COUNT = 96
OCCUPIED_COUNT = 16
TRANSFER_COUNT = 16
SQRT_STEP = 0.05

DOUBLED = 2 * ORBITAL_COUNT
PAIR = 2 * DOUBLED
WINDOW = 256
SHIFT = PAIR - WINDOW
LANES = 128
BLOCK = 16
PITCH_EXTRA = 4
VMEM_LIMIT = 60 * 1024 * 1024
F32 = jnp.float32
MESH = pl.DeviceIdType.MESH


def offsets_of(devices):
    return [0, devices - 1, 1, devices // 2]


def row_of(part, occupied, walkers):
    half = (OCCUPIED_COUNT // 2) * walkers
    return part * 2 * half + (occupied % 2) * half + (occupied // 2) * walkers


def on_diagonal(count):
    return lax.broadcasted_iota(jnp.int32, (count, count), 0) == lax.broadcasted_iota(jnp.int32, (count, count), 1)


def column_of(row):
    count = row.shape[1]
    return jnp.sum(jnp.where(on_diagonal(count), jnp.broadcast_to(row, (count, count)), 0.0), axis=1, keepdims=True)


def step_kernel(
    devices,
    groups,
    source_ref,
    transfer_ref,
    multiple_ref,
    greens_hbm,
    chol_hbm,
    fields_hbm,
    weight_ref,
    bias_ref,
    total_ref,
    greens,
    fields,
    raw,
    wide,
    chol,
    picked,
    arrived,
    dense_left,
    operand,
    product,
    tails,
    crossed,
    mine,
    theirs,
    rows_of_field,
    linear,
    summed,
    landed,
    packets,
    means,
    local_sem,
    green_send,
    green_recv,
    pair_send,
    pair_recv,
    share_send,
    share_recv,
    sum_send,
    sum_recv,
    mean_send,
    mean_recv,
):
    me = lax.axis_index("pb")
    group = lax.axis_index("walk")
    slots, _, walkers, _ = mine.shape
    vectors = chol_hbm.shape[0]
    per_vector = chol_hbm.shape[1]
    kpoints = greens.shape[0] // walkers
    tiles = per_vector // slots
    pitch = wide.shape[0] // BLOCK
    pairs = OCCUPIED_COUNT // 2
    lines = devices // 2
    parity, line = lax.rem(me, 2), me // 2
    width = bias_ref.shape[2]
    offsets = offsets_of(devices)

    def pb_peer(step):
        return {"pb": lax.rem(me + step, devices)}

    def walk_peer(step):
        return {"walk": lax.rem(group + step, groups)}

    barrier = pltpu.get_barrier_semaphore()
    for step in range(1, devices):
        pl.semaphore_signal(barrier, inc=1, device_id=pb_peer(step), device_id_type=MESH)
    for step in range(1, groups):
        pl.semaphore_signal(barrier, inc=1, device_id=walk_peer(step), device_id_type=MESH)

    green_in = pltpu.make_async_copy(greens_hbm, greens, local_sem.at[0])
    green_in.start()
    chunk = -(-vectors // (4 * BLOCK)) * BLOCK
    pieces = []
    for number, first in enumerate(range(0, vectors, chunk)):
        count = min(chunk, vectors - first)
        piece = pltpu.make_async_copy(
            chol_hbm.at[pl.ds(first, count)], raw.at[pl.ds(first, count)], local_sem.at[2 + number]
        )
        piece.start()
        pieces.append((first, count, piece))
    field_in = pltpu.make_async_copy(fields_hbm, fields, local_sem.at[1])
    field_in.start()

    green_in.wait()
    lane = lax.broadcasted_iota(jnp.int32, (walkers, walkers * kpoints), 1)
    row = lax.broadcasted_iota(jnp.int32, (walkers, walkers * kpoints), 0)
    chosen = []
    for slot in range(slots):
        requester = lax.rem(me + devices - offsets[slot], devices)
        index = lax.rem(source_ref[requester * slots + slot], kpoints)
        chosen.append(jnp.where(lane == row * kpoints + index, 1.0, 0.0))
    chosen = jnp.concatenate(chosen, 0).astype(greens.dtype)
    flat = greens.shape[1]
    span = PAIR * 2
    for first in range(0, flat, span):
        rows = jnp.dot(chosen, greens[:, first : first + span], preferred_element_type=F32).astype(greens.dtype)
        arrived[0, :, first : first + span] = rows[:walkers]
        for slot in range(1, slots):
            picked[slot - 1, :, first : first + span] = rows[slot * walkers : (slot + 1) * walkers]

    pl.semaphore_wait(barrier, devices + groups - 2)

    def green_copy(slot):
        return pltpu.make_async_remote_copy(
            src_ref=picked.at[slot - 1],
            dst_ref=arrived.at[slot],
            send_sem=green_send.at[slot - 1],
            recv_sem=green_recv.at[slot - 1],
            device_id=pb_peer(devices - offsets[slot] if slot else 0),
            device_id_type=MESH,
        )

    for slot in range(1, slots):
        green_copy(slot).start()

    def split(block, carry):
        first = pl.multiple_of(block * BLOCK, BLOCK)
        for n in range(BLOCK):
            wide[n * pitch : n * pitch + per_vector, :] = raw[first + n].astype(F32)
        for slot in range(slots):
            for tile in range(tiles):
                part = wide[pl.ds(tile * slots + slot, BLOCK, stride=pitch), :]
                chol[slot, pl.ds(first, BLOCK), tile * LANES : (tile + 1) * LANES] = part.astype(chol.dtype)
        return carry

    for first, count, piece in pieces:
        piece.wait()
        lax.fori_loop(first // BLOCK, -(-(first + count) // BLOCK), split, 0)
    field_in.wait()
    tails[...] = jnp.zeros_like(tails)
    linear[...] = jnp.zeros_like(linear)
    crossed[...] = jnp.zeros_like(crossed)

    pair_lane = lax.broadcasted_iota(jnp.int32, (walkers, PAIR), 1)
    is_real = lax.rem(pair_lane, DOUBLED) < ORBITAL_COUNT
    window_lane = lax.broadcasted_iota(jnp.int32, (walkers, WINDOW), 1)

    def arranged(slot, p):
        both = arrived[slot, :, PAIR * p : PAIR * (p + 1)].astype(F32)
        real = jnp.where(is_real, both, -both)
        imag = jnp.where(is_real, pltpu.roll(both, PAIR - ORBITAL_COUNT, 1), pltpu.roll(both, ORBITAL_COUNT, 1))
        return real, imag

    def pair_copy(slot):
        return pltpu.make_async_remote_copy(
            src_ref=mine.at[slot],
            dst_ref=theirs.at[slot],
            send_sem=pair_send.at[slot],
            recv_sem=pair_recv.at[slot],
            device_id={"pb": 2 * line + 1 - parity},
            device_id_type=MESH,
        )

    def traces(slot):
        for p in range(pairs):
            for part, value in enumerate(arranged(slot, p)):
                dense_left[part * walkers : (part + 1) * walkers, PAIR * p : PAIR * (p + 1)] = value.astype(
                    dense_left.dtype
                )
        trace = lax.dot_general(
            dense_left[...], chol[slot, :vectors, :], (((1,), (1,)), ((), ())), preferred_element_type=F32
        )
        trace = trace * multiple_ref[slot].astype(F32)
        transfer = transfer_ref[slot]
        for w in range(walkers):
            rows_of_field[w : w + 1, :] = fields[w, pl.ds(transfer, 1), :]
        mark = jnp.full((walkers, mine.shape[3]), transfer.astype(F32))
        for part in range(2):
            value = trace[part * walkers : (part + 1) * walkers]
            mine[slot, part] = mark
            mine[slot, part, :, :vectors] = value
            linear[part] += rows_of_field[...] * value
        pair_copy(slot).start()

    main = vectors // WINDOW * WINDOW
    rest_count = vectors - main

    def window_of(i):
        start = PAIR * (i // 2) + SHIFT * (i % 2)
        return slice(start, start + WINDOW)

    def exchange(slot):
        for p in range(pairs):
            for part, value in enumerate(arranged(slot, p)):
                low, high = value[:, :WINDOW], value[:, SHIFT:]
                even, odd = row_of(part, 2 * p, walkers), row_of(part, 2 * p + 1, walkers)
                last = WINDOW - DOUBLED
                operand[0, even : even + walkers, :] = jnp.where(window_lane < DOUBLED, low, 0.0).astype(operand.dtype)
                operand[1, even : even + walkers, :] = jnp.where(
                    window_lane >= last, pltpu.roll(low, last, 1), 0.0
                ).astype(operand.dtype)
                operand[0, odd : odd + walkers, :] = jnp.where(
                    window_lane < DOUBLED, pltpu.roll(high, DOUBLED, 1), 0.0
                ).astype(operand.dtype)
                operand[1, odd : odd + walkers, :] = jnp.where(window_lane >= last, high, 0.0).astype(operand.dtype)

        def times(which, right):
            return lax.dot_general(operand[which], right, (((1,), (1,)), ((), ())), preferred_element_type=F32)

        for i in range(OCCUPIED_COUNT):
            tails[i % 2, pl.ds(LANES * (i // 2), rest_count), :] = chol[slot, main:vectors, window_of(i)]
        for which in range(2):
            ends = times(which, tails[which])
            for p in range(pairs):
                product[2 * p + which, :, main : main + LANES] = ends[:, LANES * p : LANES * (p + 1)]

        def multiply(i):
            product[i, :, :main] = times(i % 2, chol[slot, :main, window_of(i)])

        def block(i, j, part):
            return product[i, pl.ds(row_of(part, j, walkers), walkers), :]

        zero = jnp.zeros((walkers, main + LANES), F32)
        off = [zero, zero]
        own = [zero, zero]
        multiply(0)
        for i in range(OCCUPIED_COUNT):
            if i + 1 < OCCUPIED_COUNT:
                multiply(i + 1)
            for part in range(2):
                here = block(i, i, part)
                own[part] = own[part] + here * here
                for j in range(i):
                    off[part] = off[part] + block(i, j, part) * block(j, i, part)
        crossed[...] += multiple_ref[slot].astype(F32) * ((own[0] - own[1]) + 2.0 * (off[0] - off[1]))[:, :vectors]

    def share_copy(step):
        owner = 2 * lax.rem(line + step, lines) + parity
        return pltpu.make_async_remote_copy(
            src_ref=summed.at[step],
            dst_ref=landed.at[step - 1],
            send_sem=share_send.at[step - 1],
            recv_sem=share_recv.at[step - 1],
            device_id={"pb": owner},
            device_id_type=MESH,
        )

    def terms_of(transfer, part):
        value = jnp.zeros((walkers, vectors), F32)
        for held in (mine, theirs):
            for slot in range(slots):
                here = held[slot, part]
                value = value + jnp.where(here[:, vectors : vectors + 1] == transfer, here[:, :vectors], 0.0)
        return value

    def share_of(step):
        owner = 2 * lax.rem(line + step, lines) + parity
        for part in range(2):
            if width % vectors == 0:
                each = width // vectors
                for index in range(each):
                    value = terms_of((owner * each + index).astype(F32), part)
                    summed[step, part, :, index * vectors : (index + 1) * vectors] = value
            else:
                per = vectors // width
                value = terms_of((owner // per).astype(F32), part)
                piece = lax.rem(owner, per)
                taken = value[:, :width]
                for index in range(1, per):
                    taken = jnp.where(piece == index, value[:, index * width : (index + 1) * width], taken)
                summed[step, part] = taken

    order = [lines // 2] + [step for step in range(1, lines) if step != lines // 2]

    def round_of(slot, carry):
        @pl.when(slot == 0)
        def _():
            traces(0)

        @pl.when(slot == 1)
        def _():
            def one(other, inner):
                pltpu.make_async_remote_copy(
                    src_ref=picked.at[other - 1],
                    dst_ref=arrived.at[other],
                    send_sem=green_send.at[other - 1],
                    recv_sem=green_recv.at[other - 1],
                    device_id={"pb": 2 * line + 1 - parity},
                    device_id_type=MESH,
                ).wait_recv()
                traces(other)
                return inner

            lax.fori_loop(1, slots, one, 0)

        exchange(slot)

        @pl.when(slot == 1)
        def _():
            for held in range(slots):
                pair_copy(held).wait_recv()
            for step in order:
                share_of(step)
                share_copy(step).start()
            share_of(0)

        return carry

    lax.fori_loop(0, slots, round_of, 0)

    weight = column_of(weight_ref[...])
    real = summed[0, 0]
    imag = summed[0, 1]
    for step in range(1, lines):
        share_copy(step).wait_recv()
        real = real + landed[step - 1, 0]
        imag = imag + landed[step - 1, 1]
    bias_ref[0] = real
    bias_ref[1] = imag
    coulomb = jnp.sum(real * real - imag * imag, axis=1, keepdims=True)
    mixed_part = jnp.sum(real * imag, axis=1, keepdims=True)
    square = SQRT_STEP * SQRT_STEP
    real_arg = SQRT_STEP * jnp.sum(linear[0], axis=1, keepdims=True) - (0.5 * square) * coulomb
    imag_arg = SQRT_STEP * jnp.sum(linear[1], axis=1, keepdims=True) - square * mixed_part
    energy_part = 0.5 * coulomb - 0.5 * jnp.sum(crossed[...], axis=1, keepdims=True)
    shape = (walkers, LANES)
    lane = lax.broadcasted_iota(jnp.int32, shape, 1)
    row = lax.broadcasted_iota(jnp.int32, shape, 0)
    values = (energy_part, real_arg, imag_arg)
    packet = jnp.zeros(shape, F32)
    for number, value in enumerate(values):
        packet = jnp.where(lane == row + number * walkers, value, packet)
    tail = len(values) * walkers
    packet = jnp.where(lane == tail, weight * energy_part, packet)
    packet = jnp.where(lane == tail + 1, weight * (1.0 / devices), packet)
    packets[me] = jnp.sum(packet, axis=0, keepdims=True)

    def send_all(held, at, count, send_sems, recv_sems, peer):
        started = []
        for step in range(1, count):
            copy = pltpu.make_async_remote_copy(
                src_ref=held.at[at],
                dst_ref=held.at[at],
                send_sem=send_sems.at[step - 1],
                recv_sem=recv_sems.at[step - 1],
                device_id=peer(step),
                device_id_type=MESH,
            )
            copy.start()
            started.append(copy)
        return started

    def take_all(held, at, count, send_sems, recv_sems, peer):
        for step in range(1, count):
            sender = lax.rem(at + count - step, count)
            pltpu.make_async_remote_copy(
                src_ref=held.at[sender],
                dst_ref=held.at[sender],
                send_sem=send_sems.at[step - 1],
                recv_sem=recv_sems.at[step - 1],
                device_id=peer(step),
                device_id_type=MESH,
            ).wait_recv()

    sums = send_all(packets, me, devices, sum_send, sum_recv, pb_peer)
    take_all(packets, me, devices, sum_send, sum_recv, pb_peer)
    total = packets[0]
    for index in range(1, devices):
        total = total + packets[index]
    means[group] = total
    sums += send_all(means, group, groups, mean_send, mean_recv, walk_peer)
    take_all(means, group, groups, mean_send, mean_recv, walk_peer)
    whole = means[0]
    for index in range(1, groups):
        whole = whole + means[index]
    lane = lax.broadcasted_iota(jnp.int32, (1, LANES), 1)
    total_ref[...] = jnp.where(lane < tail, total, whole)
    for copy in sums:
        copy.wait_send()
    for slot in range(1, slots):
        green_copy(slot).wait_send()
    for slot in range(slots):
        pair_copy(slot).wait_send()
    for step in range(1, lines):
        share_copy(step).wait_send()


def finish_kernel(sums_ref, total_ref, weight_ref, bias_ref, energy_ref, new_ref, mixed_ref):
    bias_ref[:, 0, :] = sums_ref[0]
    bias_ref[:, 1, :] = sums_ref[1]
    total = total_ref[...]
    weight = weight_ref[...]
    walkers = weight.shape[1]
    energy_ref[...] = total[:, :walkers]
    real, imag = total[:, walkers : 2 * walkers], total[:, 2 * walkers : 3 * walkers]
    new_ref[...] = weight * jnp.exp(real) * jnp.maximum(jnp.cos(imag), 0.0)
    tail = 3 * walkers
    mixed_ref[...] = total[:, tail : tail + 1] / total[:, tail + 1 : tail + 2]


def local(greens, cholesky, slot_source, block_transfer_index, slot_multiplicity, fields, weight):
    devices = lax.axis_size("pb")
    groups = lax.axis_size("walk")
    walkers, kpoints, flat = greens.shape
    slots, vectors, _ = cholesky.shape
    width = TRANSFER_COUNT * vectors // devices
    lines = devices // 2
    tiles = flat // LANES
    padded = -(-vectors // BLOCK) * BLOCK
    lanes = (vectors // LANES + 1) * LANES
    main = vectors // WINDOW * WINDOW
    rows = 2 * OCCUPIED_COUNT * walkers
    half = greens.dtype
    vmem = pl.BlockSpec(memory_space=pltpu.VMEM)
    smem = pl.BlockSpec(memory_space=pltpu.SMEM)
    hbm = pl.BlockSpec(memory_space=pl.ANY)
    dma = pltpu.SemaphoreType.DMA

    by_vector = (
        cholesky.reshape(slots, vectors, tiles, LANES).transpose(1, 2, 0, 3).reshape(vectors, tiles * slots, LANES)
    )
    sums, total = pl.pallas_call(
        functools.partial(step_kernel, devices, groups),
        out_shape=(
            jax.ShapeDtypeStruct((2, walkers, width), F32),
            jax.ShapeDtypeStruct((1, LANES), F32),
        ),
        in_specs=[smem, smem, smem, hbm, hbm, hbm, vmem],
        out_specs=(vmem,) * 2,
        scratch_shapes=[
            pltpu.VMEM((walkers * kpoints, flat), half),
            pltpu.VMEM(fields.shape, F32),
            pltpu.VMEM((padded, tiles * slots, LANES), half),
            pltpu.VMEM((BLOCK * (tiles * slots + PITCH_EXTRA), LANES), F32),
            pltpu.VMEM((slots, padded, flat), half),
            pltpu.VMEM((slots - 1, walkers, flat), half),
            pltpu.VMEM((slots, walkers, flat), half),
            pltpu.VMEM((2 * walkers, flat), half),
            pltpu.VMEM((2, rows, WINDOW), half),
            pltpu.VMEM((OCCUPIED_COUNT, rows, main + LANES), F32),
            pltpu.VMEM((2, LANES * OCCUPIED_COUNT // 2, WINDOW), half),
            pltpu.VMEM((walkers, vectors), F32),
            pltpu.VMEM((slots, 2, walkers, lanes), F32),
            pltpu.VMEM((slots, 2, walkers, lanes), F32),
            pltpu.VMEM((walkers, vectors), F32),
            pltpu.VMEM((2, walkers, vectors), F32),
            pltpu.VMEM((lines, 2, walkers, width), F32),
            pltpu.VMEM((lines - 1, 2, walkers, width), F32),
            pltpu.VMEM((devices, 1, LANES), F32),
            pltpu.VMEM((groups, 1, LANES), F32),
            dma((8,)),
            dma((slots - 1,)),
            dma((slots - 1,)),
            dma((slots,)),
            dma((slots,)),
            dma((lines - 1,)),
            dma((lines - 1,)),
            dma((devices - 1,)),
            dma((devices - 1,)),
            dma((max(groups - 1, 1),)),
            dma((max(groups - 1, 1),)),
        ],
        compiler_params=pltpu.CompilerParams(collective_id=1, has_side_effects=True, vmem_limit_bytes=VMEM_LIMIT),
        name="step",
    )(
        slot_source,
        block_transfer_index,
        slot_multiplicity,
        greens.reshape(walkers * kpoints, flat),
        by_vector,
        fields,
        weight.reshape(1, walkers),
    )
    bias, energy, new_weight, mixed = pl.pallas_call(
        finish_kernel,
        out_shape=(
            jax.ShapeDtypeStruct((walkers, 2, width), F32),
            jax.ShapeDtypeStruct((1, walkers), F32),
            jax.ShapeDtypeStruct((1, walkers), F32),
            jax.ShapeDtypeStruct((1, 1), F32),
        ),
        in_specs=[vmem] * 3,
        out_specs=(vmem,) * 4,
        name="finish",
    )(sums, total, weight.reshape(1, walkers))
    return bias, energy.reshape(walkers), new_weight.reshape(walkers), mixed.reshape(())


def solution(mesh):
    placed = (
        P("walk", "pb", None),
        P("pb", None, None),
        P(),
        P("pb"),
        P("pb"),
        P("walk", None, None),
        P("walk"),
    )
    return jax.shard_map(
        local,
        mesh=mesh,
        in_specs=placed,
        out_specs=(P("walk", None, "pb"), P("walk"), P("walk"), P()),
        check_vma=False,
    )
```

```python
import functools

import jax
import jax.numpy as jnp
from jax import lax
from jax.experimental import pallas as pl
from jax.experimental.pallas import tpu as pltpu
from jax.sharding import PartitionSpec as P

ORBITAL_COUNT = 96
OCCUPIED_COUNT = 16
TRANSFER_COUNT = 16
SQRT_STEP = 0.05

DOUBLED = 2 * ORBITAL_COUNT
PAIR = 2 * DOUBLED
WINDOW = 256
SHIFT = PAIR - WINDOW
LANES = 128
BLOCK = 16
PITCH_EXTRA = 4
VMEM_LIMIT = 60 * 1024 * 1024
F32 = jnp.float32
MESH = pl.DeviceIdType.MESH


def offsets_of(devices):
    return [0, devices - 1, 1, devices // 2]


def row_of(part, occupied, walkers):
    half = (OCCUPIED_COUNT // 2) * walkers
    return part * 2 * half + (occupied % 2) * half + (occupied // 2) * walkers


def on_diagonal(count):
    return lax.broadcasted_iota(jnp.int32, (count, count), 0) == lax.broadcasted_iota(jnp.int32, (count, count), 1)


def column_of(row):
    count = row.shape[1]
    return jnp.sum(jnp.where(on_diagonal(count), jnp.broadcast_to(row, (count, count)), 0.0), axis=1, keepdims=True)


def step_kernel(
    devices,
    groups,
    source_ref,
    transfer_ref,
    multiple_ref,
    greens_hbm,
    chol_hbm,
    fields_hbm,
    weight_ref,
    bias_ref,
    total_ref,
    greens,
    fields,
    raw,
    wide,
    chol,
    picked,
    arrived,
    dense_left,
    operand,
    product,
    tails,
    crossed,
    mine,
    theirs,
    rows_of_field,
    linear,
    summed,
    landed,
    relay,
    packets,
    means,
    local_sem,
    green_send,
    green_recv,
    pair_send,
    pair_recv,
    share_send,
    share_recv,
    relay_recv,
    sum_send,
    sum_recv,
    mean_send,
    mean_recv,
):
    me = lax.axis_index("pb")
    group = lax.axis_index("walk")
    slots, _, walkers, _ = mine.shape
    vectors = chol_hbm.shape[0]
    per_vector = chol_hbm.shape[1]
    kpoints = greens.shape[0] // walkers
    tiles = per_vector // slots
    pitch = wide.shape[0] // BLOCK
    pairs = OCCUPIED_COUNT // 2
    lines = devices // 2
    parity, line = lax.rem(me, 2), me // 2
    width = bias_ref.shape[2]
    offsets = offsets_of(devices)

    def pb_peer(step):
        return {"pb": lax.rem(me + step, devices)}

    def walk_peer(step):
        return {"walk": lax.rem(group + step, groups)}

    landed[...] = jnp.zeros_like(landed)
    barrier = pltpu.get_barrier_semaphore()
    for step in range(1, devices):
        pl.semaphore_signal(barrier, inc=1, device_id=pb_peer(step), device_id_type=MESH)
    for step in range(1, groups):
        pl.semaphore_signal(barrier, inc=1, device_id=walk_peer(step), device_id_type=MESH)

    green_in = pltpu.make_async_copy(greens_hbm, greens, local_sem.at[0])
    green_in.start()
    chunk = -(-vectors // (4 * BLOCK)) * BLOCK
    pieces = []
    for number, first in enumerate(range(0, vectors, chunk)):
        count = min(chunk, vectors - first)
        piece = pltpu.make_async_copy(
            chol_hbm.at[pl.ds(first, count)], raw.at[pl.ds(first, count)], local_sem.at[2 + number]
        )
        piece.start()
        pieces.append((first, count, piece))
    field_in = pltpu.make_async_copy(fields_hbm, fields, local_sem.at[1])
    field_in.start()

    green_in.wait()
    lane = lax.broadcasted_iota(jnp.int32, (walkers, walkers * kpoints), 1)
    row = lax.broadcasted_iota(jnp.int32, (walkers, walkers * kpoints), 0)
    chosen = []
    for slot in range(slots):
        requester = lax.rem(me + devices - offsets[slot], devices)
        index = lax.rem(source_ref[requester * slots + slot], kpoints)
        chosen.append(jnp.where(lane == row * kpoints + index, 1.0, 0.0))
    chosen = jnp.concatenate(chosen, 0).astype(greens.dtype)
    flat = greens.shape[1]
    span = PAIR * 2
    for first in range(0, flat, span):
        rows = jnp.dot(chosen, greens[:, first : first + span], preferred_element_type=F32).astype(greens.dtype)
        arrived[0, :, first : first + span] = rows[:walkers]
        for slot in range(1, slots):
            picked[slot - 1, :, first : first + span] = rows[slot * walkers : (slot + 1) * walkers]

    pl.semaphore_wait(barrier, devices + groups - 2)

    def green_copy(slot):
        return pltpu.make_async_remote_copy(
            src_ref=picked.at[slot - 1],
            dst_ref=arrived.at[slot],
            send_sem=green_send.at[slot - 1],
            recv_sem=green_recv.at[slot - 1],
            device_id=pb_peer(devices - offsets[slot] if slot else 0),
            device_id_type=MESH,
        )

    for slot in range(1, slots):
        green_copy(slot).start()

    def split(block, carry):
        first = pl.multiple_of(block * BLOCK, BLOCK)
        for n in range(BLOCK):
            wide[n * pitch : n * pitch + per_vector, :] = raw[first + n].astype(F32)
        for slot in range(slots):
            for tile in range(tiles):
                part = wide[pl.ds(tile * slots + slot, BLOCK, stride=pitch), :]
                chol[slot, pl.ds(first, BLOCK), tile * LANES : (tile + 1) * LANES] = part.astype(chol.dtype)
        return carry

    for first, count, piece in pieces:
        piece.wait()
        lax.fori_loop(first // BLOCK, -(-(first + count) // BLOCK), split, 0)
    field_in.wait()
    tails[...] = jnp.zeros_like(tails)
    linear[...] = jnp.zeros_like(linear)
    crossed[...] = jnp.zeros_like(crossed)

    pair_lane = lax.broadcasted_iota(jnp.int32, (walkers, PAIR), 1)
    is_real = lax.rem(pair_lane, DOUBLED) < ORBITAL_COUNT
    window_lane = lax.broadcasted_iota(jnp.int32, (walkers, WINDOW), 1)

    def arranged(slot, p):
        both = arrived[slot, :, PAIR * p : PAIR * (p + 1)].astype(F32)
        real = jnp.where(is_real, both, -both)
        imag = jnp.where(is_real, pltpu.roll(both, PAIR - ORBITAL_COUNT, 1), pltpu.roll(both, ORBITAL_COUNT, 1))
        return real, imag

    def pair_copy(slot):
        return pltpu.make_async_remote_copy(
            src_ref=mine.at[slot],
            dst_ref=theirs.at[slot],
            send_sem=pair_send.at[slot],
            recv_sem=pair_recv.at[slot],
            device_id={"pb": 2 * line + 1 - parity},
            device_id_type=MESH,
        )

    def traces(slot):
        for p in range(pairs):
            for part, value in enumerate(arranged(slot, p)):
                dense_left[part * walkers : (part + 1) * walkers, PAIR * p : PAIR * (p + 1)] = value.astype(
                    dense_left.dtype
                )
        trace = lax.dot_general(
            dense_left[...], chol[slot, :vectors, :], (((1,), (1,)), ((), ())), preferred_element_type=F32
        )
        trace = trace * multiple_ref[slot].astype(F32)
        transfer = transfer_ref[slot]
        for w in range(walkers):
            rows_of_field[w : w + 1, :] = fields[w, pl.ds(transfer, 1), :]
        mark = jnp.full((walkers, mine.shape[3]), transfer.astype(F32))
        for part in range(2):
            value = trace[part * walkers : (part + 1) * walkers]
            mine[slot, part] = mark
            mine[slot, part, :, :vectors] = value
            linear[part] += rows_of_field[...] * value
        pair_copy(slot).start()

    main = vectors // WINDOW * WINDOW
    rest_count = vectors - main

    def window_of(i):
        start = PAIR * (i // 2) + SHIFT * (i % 2)
        return slice(start, start + WINDOW)

    def exchange(slot):
        for p in range(pairs):
            for part, value in enumerate(arranged(slot, p)):
                low, high = value[:, :WINDOW], value[:, SHIFT:]
                even, odd = row_of(part, 2 * p, walkers), row_of(part, 2 * p + 1, walkers)
                last = WINDOW - DOUBLED
                operand[0, even : even + walkers, :] = jnp.where(window_lane < DOUBLED, low, 0.0).astype(operand.dtype)
                operand[1, even : even + walkers, :] = jnp.where(
                    window_lane >= last, pltpu.roll(low, last, 1), 0.0
                ).astype(operand.dtype)
                operand[0, odd : odd + walkers, :] = jnp.where(
                    window_lane < DOUBLED, pltpu.roll(high, DOUBLED, 1), 0.0
                ).astype(operand.dtype)
                operand[1, odd : odd + walkers, :] = jnp.where(window_lane >= last, high, 0.0).astype(operand.dtype)

        def times(which, right):
            return lax.dot_general(operand[which], right, (((1,), (1,)), ((), ())), preferred_element_type=F32)

        for i in range(OCCUPIED_COUNT):
            tails[i % 2, pl.ds(LANES * (i // 2), rest_count), :] = chol[slot, main:vectors, window_of(i)]
        for which in range(2):
            ends = times(which, tails[which])
            for p in range(pairs):
                product[2 * p + which, :, main : main + LANES] = ends[:, LANES * p : LANES * (p + 1)]

        def multiply(i):
            product[i, :, :main] = times(i % 2, chol[slot, :main, window_of(i)])

        def block(i, j, part):
            return product[i, pl.ds(row_of(part, j, walkers), walkers), :]

        zero = jnp.zeros((walkers, main + LANES), F32)
        off = [zero, zero]
        own = [zero, zero]
        multiply(0)
        for i in range(OCCUPIED_COUNT):
            if i + 1 < OCCUPIED_COUNT:
                multiply(i + 1)
            for part in range(2):
                here = block(i, i, part)
                own[part] = own[part] + here * here
                for j in range(i):
                    off[part] = off[part] + block(i, j, part) * block(j, i, part)
        crossed[...] += multiple_ref[slot].astype(F32) * ((own[0] - own[1]) + 2.0 * (off[0] - off[1]))[:, :vectors]

    def share_copy(step):
        owner = 2 * lax.rem(line + step, lines) + parity
        return pltpu.make_async_remote_copy(
            src_ref=summed.at[step],
            dst_ref=landed.at[step - 1],
            send_sem=share_send.at[step - 1],
            recv_sem=share_recv.at[step - 1],
            device_id={"pb": owner},
            device_id_type=MESH,
        )

    last_line = lines - 1

    def relay_copy(step):
        return pltpu.make_async_remote_copy(
            src_ref=summed.at[step],
            dst_ref=relay,
            send_sem=share_send.at[step - 1],
            recv_sem=relay_recv.at[0],
            device_id={"pb": 2 * jnp.where(line == 0, 1, lines - 2) + parity},
            device_id_type=MESH,
        )

    def handed_on(step):
        if lines < 4 or step not in (1, last_line):
            return None
        return line == (0 if step == last_line else last_line)

    def handed_to_me(step):
        if lines < 4 or step not in (2, lines - 2):
            return None
        if lines == 4:
            return (line == 1) | (line == 2)
        return line == (1 if step == lines - 2 else lines - 2)

    def not_sent_here(step):
        if lines < 4 or step not in (1, last_line):
            return None
        return line == (last_line if step == last_line else 0)

    def either(condition, yes, no):
        if condition is None:
            no()
            return

        @pl.when(condition)
        def _():
            yes()

        @pl.when(jnp.logical_not(condition))
        def _():
            no()

    def nothing():
        pass

    def forward(step):
        relay_copy(step).wait_recv()
        summed[step] += relay[...]
        share_copy(step).start()

    def terms_of(transfer, part):
        value = jnp.zeros((walkers, vectors), F32)
        for held in (mine, theirs):
            for slot in range(slots):
                here = held[slot, part]
                value = value + jnp.where(here[:, vectors : vectors + 1] == transfer, here[:, :vectors], 0.0)
        return value

    def share_of(step):
        owner = 2 * lax.rem(line + step, lines) + parity
        for part in range(2):
            if width % vectors == 0:
                each = width // vectors
                for index in range(each):
                    value = terms_of((owner * each + index).astype(F32), part)
                    summed[step, part, :, index * vectors : (index + 1) * vectors] = value
            else:
                per = vectors // width
                value = terms_of((owner // per).astype(F32), part)
                piece = lax.rem(owner, per)
                taken = value[:, :width]
                for index in range(1, per):
                    taken = jnp.where(piece == index, value[:, index * width : (index + 1) * width], taken)
                summed[step, part] = taken

    first_sent = [step for step in (last_line, 1) if step < lines]
    order = list(dict.fromkeys(first_sent + [lines // 2] + list(range(1, lines))))

    def round_of(slot, carry):
        @pl.when(slot == 0)
        def _():
            traces(0)

        @pl.when(slot == 1)
        def _():
            def one(other, inner):
                pltpu.make_async_remote_copy(
                    src_ref=picked.at[other - 1],
                    dst_ref=arrived.at[other],
                    send_sem=green_send.at[other - 1],
                    recv_sem=green_recv.at[other - 1],
                    device_id={"pb": 2 * line + 1 - parity},
                    device_id_type=MESH,
                ).wait_recv()
                traces(other)
                return inner

            lax.fori_loop(1, slots, one, 0)

        exchange(slot)

        @pl.when(slot == 1)
        def _():
            for held in range(slots):
                pair_copy(held).wait_recv()
            for step in order:
                share_of(step)
                if handed_on(step) is not None:
                    either(handed_on(step), lambda: relay_copy(step).start(), lambda: share_copy(step).start())
                else:
                    either(handed_to_me(step), nothing, lambda: share_copy(step).start())
            share_of(0)

        return carry

    lax.fori_loop(0, slots, round_of, 0)

    for step in range(1, lines):
        if handed_to_me(step) is not None:
            either(handed_to_me(step), lambda: forward(step), nothing)
    weight = column_of(weight_ref[...])
    real = summed[0, 0]
    imag = summed[0, 1]
    for step in range(1, lines):
        either(not_sent_here(step), nothing, lambda: share_copy(step).wait_recv())
        real = real + landed[step - 1, 0]
        imag = imag + landed[step - 1, 1]
    bias_ref[0] = real
    bias_ref[1] = imag
    coulomb = jnp.sum(real * real - imag * imag, axis=1, keepdims=True)
    mixed_part = jnp.sum(real * imag, axis=1, keepdims=True)
    square = SQRT_STEP * SQRT_STEP
    real_arg = SQRT_STEP * jnp.sum(linear[0], axis=1, keepdims=True) - (0.5 * square) * coulomb
    imag_arg = SQRT_STEP * jnp.sum(linear[1], axis=1, keepdims=True) - square * mixed_part
    energy_part = 0.5 * coulomb - 0.5 * jnp.sum(crossed[...], axis=1, keepdims=True)
    shape = (walkers, LANES)
    lane = lax.broadcasted_iota(jnp.int32, shape, 1)
    row = lax.broadcasted_iota(jnp.int32, shape, 0)
    values = (energy_part, real_arg, imag_arg)
    packet = jnp.zeros(shape, F32)
    for number, value in enumerate(values):
        packet = jnp.where(lane == row + number * walkers, value, packet)
    tail = len(values) * walkers
    packet = jnp.where(lane == tail, weight * energy_part, packet)
    packet = jnp.where(lane == tail + 1, weight * (1.0 / devices), packet)
    packets[me] = jnp.sum(packet, axis=0, keepdims=True)

    def send_all(held, at, count, send_sems, recv_sems, peer):
        started = []
        for step in range(1, count):
            copy = pltpu.make_async_remote_copy(
                src_ref=held.at[at],
                dst_ref=held.at[at],
                send_sem=send_sems.at[step - 1],
                recv_sem=recv_sems.at[step - 1],
                device_id=peer(step),
                device_id_type=MESH,
            )
            copy.start()
            started.append(copy)
        return started

    def take_all(held, at, count, send_sems, recv_sems, peer):
        for step in range(1, count):
            sender = lax.rem(at + count - step, count)
            pltpu.make_async_remote_copy(
                src_ref=held.at[sender],
                dst_ref=held.at[sender],
                send_sem=send_sems.at[step - 1],
                recv_sem=recv_sems.at[step - 1],
                device_id=peer(step),
                device_id_type=MESH,
            ).wait_recv()

    sums = send_all(packets, me, devices, sum_send, sum_recv, pb_peer)
    take_all(packets, me, devices, sum_send, sum_recv, pb_peer)
    total = packets[0]
    for index in range(1, devices):
        total = total + packets[index]
    means[group] = total
    sums += send_all(means, group, groups, mean_send, mean_recv, walk_peer)
    take_all(means, group, groups, mean_send, mean_recv, walk_peer)
    whole = means[0]
    for index in range(1, groups):
        whole = whole + means[index]
    lane = lax.broadcasted_iota(jnp.int32, (1, LANES), 1)
    total_ref[...] = jnp.where(lane < tail, total, whole)
    for copy in sums:
        copy.wait_send()
    for slot in range(1, slots):
        green_copy(slot).wait_send()
    for slot in range(slots):
        pair_copy(slot).wait_send()
    for step in range(1, lines):
        either(handed_on(step), lambda: relay_copy(step).wait_send(), lambda: share_copy(step).wait_send())


def finish_kernel(sums_ref, total_ref, weight_ref, bias_ref, energy_ref, new_ref, mixed_ref):
    bias_ref[:, 0, :] = sums_ref[0]
    bias_ref[:, 1, :] = sums_ref[1]
    total = total_ref[...]
    weight = weight_ref[...]
    walkers = weight.shape[1]
    energy_ref[...] = total[:, :walkers]
    real, imag = total[:, walkers : 2 * walkers], total[:, 2 * walkers : 3 * walkers]
    new_ref[...] = weight * jnp.exp(real) * jnp.maximum(jnp.cos(imag), 0.0)
    tail = 3 * walkers
    mixed_ref[...] = total[:, tail : tail + 1] / total[:, tail + 1 : tail + 2]


def local(greens, cholesky, slot_source, block_transfer_index, slot_multiplicity, fields, weight):
    devices = lax.axis_size("pb")
    groups = lax.axis_size("walk")
    walkers, kpoints, flat = greens.shape
    slots, vectors, _ = cholesky.shape
    width = TRANSFER_COUNT * vectors // devices
    lines = devices // 2
    tiles = flat // LANES
    padded = -(-vectors // BLOCK) * BLOCK
    lanes = (vectors // LANES + 1) * LANES
    main = vectors // WINDOW * WINDOW
    rows = 2 * OCCUPIED_COUNT * walkers
    half = greens.dtype
    vmem = pl.BlockSpec(memory_space=pltpu.VMEM)
    smem = pl.BlockSpec(memory_space=pltpu.SMEM)
    hbm = pl.BlockSpec(memory_space=pl.ANY)
    dma = pltpu.SemaphoreType.DMA

    by_vector = (
        cholesky.reshape(slots, vectors, tiles, LANES).transpose(1, 2, 0, 3).reshape(vectors, tiles * slots, LANES)
    )
    sums, total = pl.pallas_call(
        functools.partial(step_kernel, devices, groups),
        out_shape=(
            jax.ShapeDtypeStruct((2, walkers, width), F32),
            jax.ShapeDtypeStruct((1, LANES), F32),
        ),
        in_specs=[smem, smem, smem, hbm, hbm, hbm, vmem],
        out_specs=(vmem,) * 2,
        scratch_shapes=[
            pltpu.VMEM((walkers * kpoints, flat), half),
            pltpu.VMEM(fields.shape, F32),
            pltpu.VMEM((padded, tiles * slots, LANES), half),
            pltpu.VMEM((BLOCK * (tiles * slots + PITCH_EXTRA), LANES), F32),
            pltpu.VMEM((slots, padded, flat), half),
            pltpu.VMEM((slots - 1, walkers, flat), half),
            pltpu.VMEM((slots, walkers, flat), half),
            pltpu.VMEM((2 * walkers, flat), half),
            pltpu.VMEM((2, rows, WINDOW), half),
            pltpu.VMEM((OCCUPIED_COUNT, rows, main + LANES), F32),
            pltpu.VMEM((2, LANES * OCCUPIED_COUNT // 2, WINDOW), half),
            pltpu.VMEM((walkers, vectors), F32),
            pltpu.VMEM((slots, 2, walkers, lanes), F32),
            pltpu.VMEM((slots, 2, walkers, lanes), F32),
            pltpu.VMEM((walkers, vectors), F32),
            pltpu.VMEM((2, walkers, vectors), F32),
            pltpu.VMEM((lines, 2, walkers, width), F32),
            pltpu.VMEM((lines - 1, 2, walkers, width), F32),
            pltpu.VMEM((2, walkers, width), F32),
            pltpu.VMEM((devices, 1, LANES), F32),
            pltpu.VMEM((groups, 1, LANES), F32),
            dma((8,)),
            dma((slots - 1,)),
            dma((slots - 1,)),
            dma((slots,)),
            dma((slots,)),
            dma((lines - 1,)),
            dma((lines - 1,)),
            dma((1,)),
            dma((devices - 1,)),
            dma((devices - 1,)),
            dma((max(groups - 1, 1),)),
            dma((max(groups - 1, 1),)),
        ],
        compiler_params=pltpu.CompilerParams(collective_id=1, has_side_effects=True, vmem_limit_bytes=VMEM_LIMIT),
        name="step",
    )(
        slot_source,
        block_transfer_index,
        slot_multiplicity,
        greens.reshape(walkers * kpoints, flat),
        by_vector,
        fields,
        weight.reshape(1, walkers),
    )
    bias, energy, new_weight, mixed = pl.pallas_call(
        finish_kernel,
        out_shape=(
            jax.ShapeDtypeStruct((walkers, 2, width), F32),
            jax.ShapeDtypeStruct((1, walkers), F32),
            jax.ShapeDtypeStruct((1, walkers), F32),
            jax.ShapeDtypeStruct((1, 1), F32),
        ),
        in_specs=[vmem] * 3,
        out_specs=(vmem,) * 4,
        name="finish",
    )(sums, total, weight.reshape(1, walkers))
    return bias, energy.reshape(walkers), new_weight.reshape(walkers), mixed.reshape(())


def solution(mesh):
    placed = (
        P("walk", "pb", None),
        P("pb", None, None),
        P(),
        P("pb"),
        P("pb"),
        P("walk", None, None),
        P("walk"),
    )
    return jax.shard_map(
        local,
        mesh=mesh,
        in_specs=placed,
        out_specs=(P("walk", None, "pb"), P("walk"), P("walk"), P()),
        check_vma=False,
    )
```

```python
import functools

import jax
import jax.numpy as jnp
from jax import lax
from jax.experimental import pallas as pl
from jax.experimental.pallas import tpu as pltpu
from jax.sharding import PartitionSpec as P

ORBITAL_COUNT = 96
OCCUPIED_COUNT = 16
TRANSFER_COUNT = 16
SQRT_STEP = 0.05

DOUBLED = 2 * ORBITAL_COUNT
PAIR = 2 * DOUBLED
WINDOW = 256
SHIFT = PAIR - WINDOW
LANES = 128
BLOCK = 16
PITCH_EXTRA = 4
VMEM_LIMIT = 60 * 1024 * 1024
F32 = jnp.float32
MESH = pl.DeviceIdType.MESH


def offsets_of(devices):
    return [0, devices - 1, 1, devices // 2]


def row_of(part, occupied, walkers):
    half = (OCCUPIED_COUNT // 2) * walkers
    return part * 2 * half + (occupied % 2) * half + (occupied // 2) * walkers


def on_diagonal(count):
    return lax.broadcasted_iota(jnp.int32, (count, count), 0) == lax.broadcasted_iota(jnp.int32, (count, count), 1)


def column_of(row):
    count = row.shape[1]
    return jnp.sum(jnp.where(on_diagonal(count), jnp.broadcast_to(row, (count, count)), 0.0), axis=1, keepdims=True)


def step_kernel(
    devices,
    groups,
    source_ref,
    transfer_ref,
    multiple_ref,
    greens_hbm,
    chol_hbm,
    fields_hbm,
    weight_ref,
    bias_ref,
    total_ref,
    greens,
    fields,
    raw,
    wide,
    chol,
    picked,
    arrived,
    dense_left,
    operand,
    product,
    tails,
    crossed,
    mine,
    theirs,
    rows_of_field,
    linear,
    summed,
    landed,
    packets,
    means,
    local_sem,
    green_send,
    green_recv,
    pair_send,
    pair_recv,
    share_send,
    share_recv,
    sum_send,
    sum_recv,
    mean_send,
    mean_recv,
):
    me = lax.axis_index("pb")
    group = lax.axis_index("walk")
    slots, _, walkers, _ = mine.shape
    vectors = chol_hbm.shape[0]
    per_vector = chol_hbm.shape[1]
    kpoints = greens.shape[0] // walkers
    tiles = per_vector // slots
    pitch = wide.shape[0] // BLOCK
    pairs = OCCUPIED_COUNT // 2
    lines = devices // 2
    parity, line = lax.rem(me, 2), me // 2
    width = bias_ref.shape[2]
    offsets = offsets_of(devices)

    def pb_peer(step):
        return {"pb": lax.rem(me + step, devices)}

    def walk_peer(step):
        return {"walk": lax.rem(group + step, groups)}

    barrier = pltpu.get_barrier_semaphore()
    for step in range(1, devices):
        pl.semaphore_signal(barrier, inc=1, device_id=pb_peer(step), device_id_type=MESH)
    for step in range(1, groups):
        pl.semaphore_signal(barrier, inc=1, device_id=walk_peer(step), device_id_type=MESH)

    green_in = pltpu.make_async_copy(greens_hbm, greens, local_sem.at[0])
    green_in.start()
    chunk = -(-vectors // (4 * BLOCK)) * BLOCK
    pieces = []
    for number, first in enumerate(range(0, vectors, chunk)):
        count = min(chunk, vectors - first)
        piece = pltpu.make_async_copy(
            chol_hbm.at[pl.ds(first, count)], raw.at[pl.ds(first, count)], local_sem.at[2 + number]
        )
        piece.start()
        pieces.append((first, count, piece))
    field_in = pltpu.make_async_copy(fields_hbm, fields, local_sem.at[1])
    field_in.start()

    green_in.wait()
    lane = lax.broadcasted_iota(jnp.int32, (walkers, walkers * kpoints), 1)
    row = lax.broadcasted_iota(jnp.int32, (walkers, walkers * kpoints), 0)
    chosen = []
    for slot in range(slots):
        requester = lax.rem(me + devices - offsets[slot], devices)
        index = lax.rem(source_ref[requester * slots + slot], kpoints)
        chosen.append(jnp.where(lane == row * kpoints + index, 1.0, 0.0))
    chosen = jnp.concatenate(chosen, 0).astype(greens.dtype)
    flat = greens.shape[1]
    span = PAIR * 2
    for first in range(0, flat, span):
        rows = jnp.dot(chosen, greens[:, first : first + span], preferred_element_type=F32).astype(greens.dtype)
        arrived[0, :, first : first + span] = rows[:walkers]
        for slot in range(1, slots):
            picked[slot - 1, :, first : first + span] = rows[slot * walkers : (slot + 1) * walkers]

    pl.semaphore_wait(barrier, devices + groups - 2)

    def green_copy(slot):
        return pltpu.make_async_remote_copy(
            src_ref=picked.at[slot - 1],
            dst_ref=arrived.at[slot],
            send_sem=green_send.at[slot - 1],
            recv_sem=green_recv.at[slot - 1],
            device_id=pb_peer(devices - offsets[slot] if slot else 0),
            device_id_type=MESH,
        )

    for slot in range(1, slots):
        green_copy(slot).start()

    def split(block, carry):
        first = pl.multiple_of(block * BLOCK, BLOCK)
        for n in range(BLOCK):
            wide[n * pitch : n * pitch + per_vector, :] = raw[first + n].astype(F32)
        for slot in range(slots):
            for tile in range(tiles):
                part = wide[pl.ds(tile * slots + slot, BLOCK, stride=pitch), :]
                chol[slot, pl.ds(first, BLOCK), tile * LANES : (tile + 1) * LANES] = part.astype(chol.dtype)
        return carry

    for first, count, piece in pieces:
        piece.wait()
        lax.fori_loop(first // BLOCK, -(-(first + count) // BLOCK), split, 0)
    field_in.wait()
    tails[...] = jnp.zeros_like(tails)
    linear[...] = jnp.zeros_like(linear)
    crossed[...] = jnp.zeros_like(crossed)

    pair_lane = lax.broadcasted_iota(jnp.int32, (walkers, PAIR), 1)
    is_real = lax.rem(pair_lane, DOUBLED) < ORBITAL_COUNT
    window_lane = lax.broadcasted_iota(jnp.int32, (walkers, WINDOW), 1)

    def arranged(slot, p):
        both = arrived[slot, :, PAIR * p : PAIR * (p + 1)].astype(F32)
        real = jnp.where(is_real, both, -both)
        imag = jnp.where(is_real, pltpu.roll(both, PAIR - ORBITAL_COUNT, 1), pltpu.roll(both, ORBITAL_COUNT, 1))
        return real, imag

    def pair_copy(slot):
        return pltpu.make_async_remote_copy(
            src_ref=mine.at[slot],
            dst_ref=theirs.at[slot],
            send_sem=pair_send.at[slot],
            recv_sem=pair_recv.at[slot],
            device_id={"pb": 2 * line + 1 - parity},
            device_id_type=MESH,
        )

    def traces(slot):
        for p in range(pairs):
            for part, value in enumerate(arranged(slot, p)):
                dense_left[part * walkers : (part + 1) * walkers, PAIR * p : PAIR * (p + 1)] = value.astype(
                    dense_left.dtype
                )
        trace = lax.dot_general(
            dense_left[...], chol[slot, :vectors, :], (((1,), (1,)), ((), ())), preferred_element_type=F32
        )
        trace = trace * multiple_ref[slot].astype(F32)
        transfer = transfer_ref[slot]
        for w in range(walkers):
            rows_of_field[w : w + 1, :] = fields[w, pl.ds(transfer, 1), :]
        mark = jnp.full((walkers, mine.shape[3]), transfer.astype(F32))
        for part in range(2):
            value = trace[part * walkers : (part + 1) * walkers]
            mine[slot, part] = mark
            mine[slot, part, :, :vectors] = value
            linear[part] += rows_of_field[...] * value
        pair_copy(slot).start()

    main = vectors // WINDOW * WINDOW
    rest_count = vectors - main

    def window_of(i):
        start = PAIR * (i // 2) + SHIFT * (i % 2)
        return slice(start, start + WINDOW)

    def exchange(slot):
        for p in range(pairs):
            for part, value in enumerate(arranged(slot, p)):
                low, high = value[:, :WINDOW], value[:, SHIFT:]
                even, odd = row_of(part, 2 * p, walkers), row_of(part, 2 * p + 1, walkers)
                last = WINDOW - DOUBLED
                operand[0, even : even + walkers, :] = jnp.where(window_lane < DOUBLED, low, 0.0).astype(operand.dtype)
                operand[1, even : even + walkers, :] = jnp.where(
                    window_lane >= last, pltpu.roll(low, last, 1), 0.0
                ).astype(operand.dtype)
                operand[0, odd : odd + walkers, :] = jnp.where(
                    window_lane < DOUBLED, pltpu.roll(high, DOUBLED, 1), 0.0
                ).astype(operand.dtype)
                operand[1, odd : odd + walkers, :] = jnp.where(window_lane >= last, high, 0.0).astype(operand.dtype)

        def times(which, right):
            return lax.dot_general(operand[which], right, (((1,), (1,)), ((), ())), preferred_element_type=F32)

        for i in range(OCCUPIED_COUNT):
            tails[i % 2, pl.ds(LANES * (i // 2), rest_count), :] = chol[slot, main:vectors, window_of(i)]
        for which in range(2):
            ends = times(which, tails[which])
            for p in range(pairs):
                product[2 * p + which, :, main : main + LANES] = ends[:, LANES * p : LANES * (p + 1)]

        def multiply(i):
            product[i, :, :main] = times(i % 2, chol[slot, :main, window_of(i)])

        def block(i, j, part):
            return product[i, pl.ds(row_of(part, j, walkers), walkers), :]

        zero = jnp.zeros((walkers, main + LANES), F32)
        off = [zero, zero]
        own = [zero, zero]
        multiply(0)
        for i in range(OCCUPIED_COUNT):
            if i + 1 < OCCUPIED_COUNT:
                multiply(i + 1)
            for part in range(2):
                here = block(i, i, part)
                own[part] = own[part] + here * here
                for j in range(i):
                    off[part] = off[part] + block(i, j, part) * block(j, i, part)
        crossed[...] += multiple_ref[slot].astype(F32) * ((own[0] - own[1]) + 2.0 * (off[0] - off[1]))[:, :vectors]

    def share_copy(step):
        owner = 2 * lax.rem(line + step, lines) + parity
        return pltpu.make_async_remote_copy(
            src_ref=summed.at[step],
            dst_ref=landed.at[step - 1],
            send_sem=share_send.at[step - 1],
            recv_sem=share_recv.at[step - 1],
            device_id={"pb": owner},
            device_id_type=MESH,
        )

    def terms_of(transfer, part):
        value = jnp.zeros((walkers, vectors), F32)
        for held in (mine, theirs):
            for slot in range(slots):
                here = held[slot, part]
                value = value + jnp.where(here[:, vectors : vectors + 1] == transfer, here[:, :vectors], 0.0)
        return value

    def share_of(step):
        owner = 2 * lax.rem(line + step, lines) + parity
        for part in range(2):
            if width % vectors == 0:
                each = width // vectors
                for index in range(each):
                    value = terms_of((owner * each + index).astype(F32), part)
                    summed[step, part, :, index * vectors : (index + 1) * vectors] = value
            else:
                per = vectors // width
                value = terms_of((owner // per).astype(F32), part)
                piece = lax.rem(owner, per)
                taken = value[:, :width]
                for index in range(1, per):
                    taken = jnp.where(piece == index, value[:, index * width : (index + 1) * width], taken)
                summed[step, part] = taken

    order = [lines // 2] + [step for step in range(1, lines) if step != lines // 2]

    def round_of(slot, carry):
        @pl.when(slot == 0)
        def _():
            traces(0)

        @pl.when(slot == 1)
        def _():
            def one(other, inner):
                pltpu.make_async_remote_copy(
                    src_ref=picked.at[other - 1],
                    dst_ref=arrived.at[other],
                    send_sem=green_send.at[other - 1],
                    recv_sem=green_recv.at[other - 1],
                    device_id={"pb": 2 * line + 1 - parity},
                    device_id_type=MESH,
                ).wait_recv()
                traces(other)
                return inner

            lax.fori_loop(1, slots, one, 0)

        exchange(slot)

        @pl.when(slot == 1)
        def _():
            for held in range(slots):
                pair_copy(held).wait_recv()
            for step in order:
                share_of(step)
                share_copy(step).start()
            share_of(0)

        return carry

    lax.fori_loop(0, slots, round_of, 0)

    weight = column_of(weight_ref[...])
    linear_real = SQRT_STEP * jnp.sum(linear[0], axis=1, keepdims=True)
    linear_imag = SQRT_STEP * jnp.sum(linear[1], axis=1, keepdims=True)
    half_cross = 0.5 * jnp.sum(crossed[...], axis=1, keepdims=True)
    real = summed[0, 0]
    imag = summed[0, 1]
    for step in range(1, lines):
        share_copy(step).wait_recv()
        real = real + landed[step - 1, 0]
        imag = imag + landed[step - 1, 1]
    summed[0, 0] = real
    summed[0, 1] = imag
    bias_out = pltpu.make_async_copy(summed.at[0], bias_ref, local_sem.at[7])
    coulomb = jnp.sum(real * real - imag * imag, axis=1, keepdims=True)
    mixed_part = jnp.sum(real * imag, axis=1, keepdims=True)
    square = SQRT_STEP * SQRT_STEP
    real_arg = linear_real - (0.5 * square) * coulomb
    imag_arg = linear_imag - square * mixed_part
    energy_part = 0.5 * coulomb - half_cross
    shape = (walkers, LANES)
    lane = lax.broadcasted_iota(jnp.int32, shape, 1)
    row = lax.broadcasted_iota(jnp.int32, shape, 0)
    values = (energy_part, real_arg, imag_arg)
    packet = jnp.zeros(shape, F32)
    for number, value in enumerate(values):
        packet = jnp.where(lane == row + number * walkers, value, packet)
    tail = len(values) * walkers
    packet = jnp.where(lane == tail, weight * energy_part, packet)
    packet = jnp.where(lane == tail + 1, weight * (1.0 / devices), packet)
    packets[me] = jnp.sum(packet, axis=0, keepdims=True)

    def send_all(held, at, count, send_sems, recv_sems, peer):
        started = []
        for step in range(1, count):
            copy = pltpu.make_async_remote_copy(
                src_ref=held.at[at],
                dst_ref=held.at[at],
                send_sem=send_sems.at[step - 1],
                recv_sem=recv_sems.at[step - 1],
                device_id=peer(step),
                device_id_type=MESH,
            )
            copy.start()
            started.append(copy)
        return started

    def take_all(held, at, count, send_sems, recv_sems, peer):
        for step in range(1, count):
            sender = lax.rem(at + count - step, count)
            pltpu.make_async_remote_copy(
                src_ref=held.at[sender],
                dst_ref=held.at[sender],
                send_sem=send_sems.at[step - 1],
                recv_sem=recv_sems.at[step - 1],
                device_id=peer(step),
                device_id_type=MESH,
            ).wait_recv()

    bias_out.start()
    sums = send_all(packets, me, devices, sum_send, sum_recv, pb_peer)
    take_all(packets, me, devices, sum_send, sum_recv, pb_peer)
    total = packets[0]
    for index in range(1, devices):
        total = total + packets[index]
    means[group] = total
    sums += send_all(means, group, groups, mean_send, mean_recv, walk_peer)
    take_all(means, group, groups, mean_send, mean_recv, walk_peer)
    whole = means[0]
    for index in range(1, groups):
        whole = whole + means[index]
    lane = lax.broadcasted_iota(jnp.int32, (1, LANES), 1)
    total_ref[...] = jnp.where(lane < tail, total, whole)
    bias_out.wait()
    for copy in sums:
        copy.wait_send()
    for slot in range(1, slots):
        green_copy(slot).wait_send()
    for slot in range(slots):
        pair_copy(slot).wait_send()
    for step in range(1, lines):
        share_copy(step).wait_send()


def finish_kernel(sums_ref, total_ref, weight_ref, bias_ref, energy_ref, new_ref, mixed_ref):
    bias_ref[:, 0, :] = sums_ref[0]
    bias_ref[:, 1, :] = sums_ref[1]
    total = total_ref[...]
    weight = weight_ref[...]
    walkers = weight.shape[1]
    energy_ref[...] = total[:, :walkers]
    real, imag = total[:, walkers : 2 * walkers], total[:, 2 * walkers : 3 * walkers]
    new_ref[...] = weight * jnp.exp(real) * jnp.maximum(jnp.cos(imag), 0.0)
    tail = 3 * walkers
    mixed_ref[...] = total[:, tail : tail + 1] / total[:, tail + 1 : tail + 2]


def local(greens, cholesky, slot_source, block_transfer_index, slot_multiplicity, fields, weight):
    devices = lax.axis_size("pb")
    groups = lax.axis_size("walk")
    walkers, kpoints, flat = greens.shape
    slots, vectors, _ = cholesky.shape
    width = TRANSFER_COUNT * vectors // devices
    lines = devices // 2
    tiles = flat // LANES
    padded = -(-vectors // BLOCK) * BLOCK
    lanes = (vectors // LANES + 1) * LANES
    main = vectors // WINDOW * WINDOW
    rows = 2 * OCCUPIED_COUNT * walkers
    half = greens.dtype
    vmem = pl.BlockSpec(memory_space=pltpu.VMEM)
    smem = pl.BlockSpec(memory_space=pltpu.SMEM)
    hbm = pl.BlockSpec(memory_space=pl.ANY)
    dma = pltpu.SemaphoreType.DMA

    by_vector = (
        cholesky.reshape(slots, vectors, tiles, LANES).transpose(1, 2, 0, 3).reshape(vectors, tiles * slots, LANES)
    )
    sums, total = pl.pallas_call(
        functools.partial(step_kernel, devices, groups),
        out_shape=(
            jax.ShapeDtypeStruct((2, walkers, width), F32),
            jax.ShapeDtypeStruct((1, LANES), F32),
        ),
        in_specs=[smem, smem, smem, hbm, hbm, hbm, vmem],
        out_specs=(hbm, vmem),
        scratch_shapes=[
            pltpu.VMEM((walkers * kpoints, flat), half),
            pltpu.VMEM(fields.shape, F32),
            pltpu.VMEM((padded, tiles * slots, LANES), half),
            pltpu.VMEM((BLOCK * (tiles * slots + PITCH_EXTRA), LANES), F32),
            pltpu.VMEM((slots, padded, flat), half),
            pltpu.VMEM((slots - 1, walkers, flat), half),
            pltpu.VMEM((slots, walkers, flat), half),
            pltpu.VMEM((2 * walkers, flat), half),
            pltpu.VMEM((2, rows, WINDOW), half),
            pltpu.VMEM((OCCUPIED_COUNT, rows, main + LANES), F32),
            pltpu.VMEM((2, LANES * OCCUPIED_COUNT // 2, WINDOW), half),
            pltpu.VMEM((walkers, vectors), F32),
            pltpu.VMEM((slots, 2, walkers, lanes), F32),
            pltpu.VMEM((slots, 2, walkers, lanes), F32),
            pltpu.VMEM((walkers, vectors), F32),
            pltpu.VMEM((2, walkers, vectors), F32),
            pltpu.VMEM((lines, 2, walkers, width), F32),
            pltpu.VMEM((lines - 1, 2, walkers, width), F32),
            pltpu.VMEM((devices, 1, LANES), F32),
            pltpu.VMEM((groups, 1, LANES), F32),
            dma((8,)),
            dma((slots - 1,)),
            dma((slots - 1,)),
            dma((slots,)),
            dma((slots,)),
            dma((lines - 1,)),
            dma((lines - 1,)),
            dma((devices - 1,)),
            dma((devices - 1,)),
            dma((max(groups - 1, 1),)),
            dma((max(groups - 1, 1),)),
        ],
        compiler_params=pltpu.CompilerParams(collective_id=1, has_side_effects=True, vmem_limit_bytes=VMEM_LIMIT),
        name="step",
    )(
        slot_source,
        block_transfer_index,
        slot_multiplicity,
        greens.reshape(walkers * kpoints, flat),
        by_vector,
        fields,
        weight.reshape(1, walkers),
    )
    bias, energy, new_weight, mixed = pl.pallas_call(
        finish_kernel,
        out_shape=(
            jax.ShapeDtypeStruct((walkers, 2, width), F32),
            jax.ShapeDtypeStruct((1, walkers), F32),
            jax.ShapeDtypeStruct((1, walkers), F32),
            jax.ShapeDtypeStruct((1, 1), F32),
        ),
        in_specs=[vmem] * 3,
        out_specs=(vmem,) * 4,
        name="finish",
    )(sums, total, weight.reshape(1, walkers))
    return bias, energy.reshape(walkers), new_weight.reshape(walkers), mixed.reshape(())


def solution(mesh):
    placed = (
        P("walk", "pb", None),
        P("pb", None, None),
        P(),
        P("pb"),
        P("pb"),
        P("walk", None, None),
        P("walk"),
    )
    return jax.shard_map(
        local,
        mesh=mesh,
        in_specs=placed,
        out_specs=(P("walk", None, "pb"), P("walk"), P("walk"), P()),
        check_vma=False,
    )
```
